768 devices in a mesh: dp: 12 (over z), seq: 64 (over y, x, core).
Axes of the slice: x: 4, y: 8, z: 12, core: 2. Of those that a mesh axis runs over, the one named last changes fastest.
Arguments:
- hidden: bfloat16 [12, 16384, 1024], P('dp', 'seq'), may hold values from -6 to 6
- segment_ids: int32 [12, 16384], P('dp'), may hold values from 0 to 255, never falling along the last dimension, each value on 1 to 512 neighbouring positions
- kernel: float32 [31, 1024], replicated, may hold values from -1 to 1
- norm_gain: float32 [1024], replicated, may hold values from 0.5 to 1.5
- projection: bfloat16 [1024, 1024], replicated, may hold values from -0.1875 to 0.1875
- cotangent: bfloat16 [12, 16384, 1024], P('dp', 'seq'), may hold values from -16 to 16
Outputs:
- conv_out: bfloat16 [12, 16384, 1024], P('dp', 'seq')
- grad_hidden: bfloat16 [12, 16384, 1024], P('dp', 'seq')
- grad_projection: float32 [1024, 1024], P('seq')
- grad_kernel: float32 [1024, 31], P('seq')
- grad_gain: float32 [1024], P('seq')
The draws below stay inside these ranges and needn't reach their ends.
Inputs may be any that keep to these rules, and one draw needn't show every extreme that they name: `segment_ids`: within a row utterance numbers never fall, every number 0 to 255 occurs, each utterance spans 1 to 512 frames and one spans exactly 512.
All inputs are finite; a program needn't handle non-finite values.
Results may differ from the reference program's by a relative error of at most 0.005.
Values may be sent and summed in bfloat16 or wider, within the bound.
No kernel may reach another device: no remote copies, remote signals or barrier semaphores. Data moves between devices by JAX's collectives and lax.ppermute only.
A program may use at most 64 MiB of HBM per device.

```python
import math
import jax
import jax.numpy as jnp
import numpy as np
from jax import lax

D = 1024
KERNEL = 31
FRAMES = 16384
UTTS = 256
SPAN = 512
N_DP = 12


def spiked(result, stream_key, source, target, parts, factor):
    def block_of(position):
        return (jnp.arange(result.shape[position]) // (result.shape[position] // parts)).reshape((-1,) + (1,) * (result.ndim - 1 - position))

    near = jax.random.permutation(stream_key, parts)[block_of(target)]
    other_side = (block_of(target) + parts // 2) % parts
    return jnp.where((block_of(source) == near) | (block_of(source) == other_side), factor * result, result)


def levels(key, dims, cuts, least, high):
    def one(position, parts):
        draws = jax.random.uniform(jax.random.fold_in(jax.random.fold_in(key, 6), position), (parts,), jnp.float32, least / len(cuts), high / len(cuts))
        return jnp.repeat(jnp.exp(draws), dims[position] // parts).reshape((-1,) + (1,) * (len(dims) - position - 1))

    factor_of = one(*cuts[0])
    for cut in cuts[1:]:
        factor_of = factor_of * one(*cut)
    return factor_of


def profile(amount, total, most, skew):
    portions = [(1 << 20) // math.isqrt(grade ** skew) + 1 for grade in range(2, amount + 1)]
    rest, given = total - most - (amount - 1), [1] * (amount - 1)
    while rest > 0:
        free = [i for i in range(amount - 1) if given[i] < most]
        pool, budget = sum([portions[i] for i in free]), rest
        for i in free:
            extra = min(most - given[i], max(1, budget * portions[i] // pool), rest)
            given[i] = given[i] + extra
            rest = rest - extra
    return np.array([most] + given)


def ragged(stream_key, amount, total, most, skew):
    if amount == 2:
        one = jax.random.randint(stream_key, (), max(1, total - most), min(most, total - 1) + 1)
        return jnp.stack([one, total - one])
    sizes = jnp.asarray(profile(amount, total, most, skew), jnp.int32)
    couples = (amount - 1) // 2
    giver, sink = sizes[1:1 + 2 * couples:2], sizes[2:2 + 2 * couples:2]
    room = jnp.minimum(giver - 1, most - sink)
    passed = jax.random.randint(jax.random.fold_in(stream_key, 1), (couples,), 0, 1 << 20) % (room + 1)
    sizes = sizes.at[1:1 + 2 * couples:2].set(giver - passed).at[2:2 + 2 * couples:2].set(sink + passed)
    return sizes[jax.random.permutation(jax.random.fold_in(stream_key, 2), amount)]


def noise(stream_key, dims, spread, most, cuts=(), held_as=jnp.bfloat16):
    entries = jax.random.normal(stream_key, dims, jnp.float32) * spread
    if len(cuts) > 0:
        entries = levels(stream_key, dims, cuts, -0.22, 0.18) * entries
    return jnp.clip(entries, min=-most, max=most).astype(held_as)


def gaussian_with(stream_key, shape, scale, limit, shards, heavy, kind=jnp.bfloat16):
    result = scale * jax.random.normal(stream_key, shape, jnp.float32)
    if shards:
        result = result * levels(stream_key, shape, shards, -0.22, 0.18)
    return jnp.clip(spiked(result, jax.random.fold_in(stream_key, 3), *heavy), -limit, limit).astype(kind)


def setup_inputs(seed: int = 0) -> dict:
    key_of = jax.random.split(jax.random.key(seed), 7)
    hidden = noise(key_of[0], (N_DP, FRAMES, D), 1.0, 6.0, ((0, 12), (1, 64)))
    segment_ids = jax.vmap(lambda own: jnp.searchsorted(jnp.cumsum(ragged(own, UTTS, FRAMES, SPAN, 2)), jnp.arange(FRAMES), side="right"))(jax.random.split(key_of[1], N_DP)).reshape((N_DP, FRAMES)).astype(jnp.int32)
    kernel = noise(key_of[2], (KERNEL, D), KERNEL ** -0.5, 1.0, (), jnp.float32)
    norm_gain = jnp.clip(1.0 + 0.1 * jax.random.normal(key_of[3], (D,), jnp.float32), 0.5, 1.5)
    projection = noise(key_of[4], (D, D), D ** -0.5, 0.1875)
    cotangent = gaussian_with(key_of[5], (N_DP, FRAMES, D), 1.0, 16.0, ((0, 12), (1, 64)), (1, 2, 64, 4.0))
    return dict(hidden=hidden, segment_ids=segment_ids, kernel=kernel, norm_gain=norm_gain, projection=projection, cotangent=cotangent)


EPS = 1e-05

def depth_forward(padded, segs, kernel, length):
    reach = KERNEL // 2
    total = jnp.zeros((length, kernel.shape[1]), jnp.float32)
    centre = segs[reach:reach + length]
    for offset in range(KERNEL):
        same = (segs[offset:offset + length] == centre).astype(jnp.float32)[:, None]
        total = total + kernel[offset] * padded[offset:offset + length].astype(jnp.float32) * same
    return total

def kernel_terms(grad, padded, segs, length):
    reach = KERNEL // 2
    centre = segs[reach:reach + length]
    rows_out = []
    for offset in range(KERNEL):
        same = (segs[offset:offset + length] == centre).astype(jnp.float32)[:, None]
        rows_out.append(lax.optimization_barrier(jnp.sum(grad * padded[offset:offset + length].astype(jnp.float32) * same, 0)))
    return jnp.stack(rows_out, 0)

def spread_back(grid, segs, kernel, length):
    reach = KERNEL // 2
    total = jnp.zeros((length, kernel.shape[1]), jnp.float32)
    centre = segs[reach:reach + length]
    for offset in range(KERNEL):
        lower = 2 * reach - offset
        same = (segs[lower:lower + length] == centre).astype(jnp.float32)[:, None]
        total = total + kernel[offset] * grid[lower:lower + length] * same
    return total

def norm_forward(mixed, norm_gain):
    centred = mixed - lax.optimization_barrier(jnp.mean(mixed, -1, keepdims=True))
    variance = lax.optimization_barrier(jnp.mean(centred * centred, -1, keepdims=True))
    scale_inv = lax.rsqrt(variance + EPS)
    normed = centred * scale_inv
    gated = normed * norm_gain
    sigma = jax.nn.sigmoid(gated)
    act = (gated * sigma).astype(jnp.bfloat16)
    return (normed, scale_inv, gated, sigma, act)

def norm_backward(grad_act, normed, scale_inv, gated, sigma, norm_gain):
    grad_gated = grad_act * sigma * (1.0 + gated * (1.0 - sigma))
    grad_normed = grad_gated * norm_gain
    grad_mixed = scale_inv * (grad_normed - lax.optimization_barrier(jnp.mean(grad_normed, -1, keepdims=True)) - normed * lax.optimization_barrier(jnp.mean(grad_normed * normed, -1, keepdims=True)))
    return (grad_gated, grad_mixed)

def reference(hidden, segment_ids, kernel, norm_gain, projection, cotangent):
    reach = KERNEL // 2

    def one_row(items):
        frames_row, seg_row, grad_out = items
        padded_in = jnp.pad(frames_row, ((reach, reach), (0, 0)))
        seg_pad = jnp.pad(seg_row, reach, constant_values=-1)
        mixed = depth_forward(padded_in, seg_pad, kernel, FRAMES)
        normed, scale_inv, gated, sigma, act = norm_forward(mixed, norm_gain)
        conv_out = jnp.dot(act, projection.T, preferred_element_type=jnp.float32).astype(jnp.bfloat16)
        grad_act = jnp.dot(grad_out, projection, preferred_element_type=jnp.float32)
        grad_gated, grad_mixed = norm_backward(grad_act, normed, scale_inv, gated, sigma, norm_gain)
        kernel_grad = kernel_terms(grad_mixed, padded_in, seg_pad, FRAMES)
        gain_grad = lax.optimization_barrier(jnp.sum(grad_gated * normed, 0))
        grad_padded = jnp.pad(grad_mixed, ((reach, reach), (0, 0)))
        grad_frames = spread_back(grad_padded, seg_pad, kernel, FRAMES).astype(jnp.bfloat16)
        weight_grad = jnp.dot(grad_out.T, act, preferred_element_type=jnp.float32)
        return (conv_out, grad_frames, weight_grad, kernel_grad, gain_grad)
    conv_out, grad_hidden, weight_grad, kernel_grad, gain_grad = lax.map(one_row, (hidden, segment_ids, cotangent))
    factor = 1.0 / math.sqrt(FRAMES * N_DP)
    grad_projection = lax.optimization_barrier(jnp.sum(weight_grad, 0)) * factor
    grad_kernel = lax.optimization_barrier(jnp.sum(kernel_grad, 0)).T * factor
    grad_gain = lax.optimization_barrier(jnp.sum(gain_grad, 0)) * factor
    return (conv_out, grad_hidden, grad_projection, grad_kernel, grad_gain)
```

```python
import math
from functools import partial

import jax
import jax.numpy as jnp
from jax import lax
from jax.experimental import pallas as pl
from jax.experimental.pallas import tpu as pltpu
from jax.sharding import Mesh
from jax.sharding import PartitionSpec as P


EPS = 1e-05
LANES = 128
HALO = 16
ROWS = 32
BF = jnp.bfloat16
F32 = jnp.float32


def call(kernel, outs, scratch=(), flops=0, moved=0, trans=0, smem=()):
    def run(*args):
        specs = [
            pl.BlockSpec(memory_space=pltpu.SMEM if i in smem else pltpu.VMEM)
            for i in range(len(args))
        ]
        return pl.pallas_call(
            kernel,
            out_shape=outs,
            in_specs=specs,
            out_specs=jax.tree.map(lambda _: pl.BlockSpec(memory_space=pltpu.VMEM), outs),
            scratch_shapes=list(scratch),
            compiler_params=pltpu.CompilerParams(vmem_limit_bytes=18 * 1024 * 1024),
            cost_estimate=pl.CostEstimate(flops=flops, bytes_accessed=moved, transcendentals=trans),
        )(*args)

    return run


def deal(core, b, turned, own, cols, mine_ref, other_ref):
    pairs = LANES // (2 * own)
    rows = mine_ref.shape[0] // own // cols
    for j in range(pairs):
        even = turned[2 * own * j : 2 * own * j + own]
        odd = turned[2 * own * j + own : 2 * own * j + 2 * own]
        y, x = divmod(b * pairs + j, cols)
        at = (x * rows + y) * own
        mine_ref[at : at + own, :] = jnp.where(core == 0, even, odd)
        other_ref[at : at + own, :] = jnp.where(core == 0, odd, even)


def split_kernel(own, cols, core_ref, cot_ref, mine_ref, other_ref):
    for b in range(cot_ref.shape[1] // LANES):
        turned = cot_ref[:, b * LANES : (b + 1) * LANES].T
        deal(core_ref[0], b, turned, own, cols, mine_ref, other_ref)


def spread(dst, before, middle, after):
    blocks, rows = dst.shape[0], dst.shape[1]
    for b in range(blocks):
        lanes = slice(b * LANES, (b + 1) * LANES)
        dst[b, 0:HALO, :] = before[:, lanes].astype(F32)
        dst[b, HALO : rows - HALO, :] = middle[:, lanes].astype(F32)
        dst[b, rows - HALO : rows, :] = after[:, lanes].astype(F32)


def forward_kernel(hid_ref, bef_ref, aft_ref, seg_ref, kern_ref, gain_ref, act_ref, norm_ref, inv_ref, win):
    taps, width = kern_ref.shape
    length = hid_ref.shape[0]
    blocks = width // LANES
    spread(win, bef_ref, hid_ref, aft_ref)

    def step(i, carry):
        r0 = pl.multiple_of(i * ROWS, ROWS)
        centre = seg_ref[pl.ds(r0 + HALO, ROWS), :]
        acc = [jnp.zeros((ROWS, LANES), F32) for _ in range(blocks)]
        for k in range(taps):
            same = seg_ref[pl.ds(r0 + k + 1, ROWS), :] == centre
            for b in range(blocks):
                w = kern_ref[k : k + 1, b * LANES : (b + 1) * LANES]
                term = win[b, pl.ds(r0 + k + 1, ROWS), :] * w
                acc[b] = acc[b] + jnp.where(same, term, 0.0)
        total = acc[0]
        for b in range(1, blocks):
            total = total + acc[b]
        mean = jnp.sum(total, axis=1, keepdims=True) * (1.0 / width)
        acc = [a - mean for a in acc]
        total = acc[0] * acc[0]
        for b in range(1, blocks):
            total = total + acc[b] * acc[b]
        inv = lax.rsqrt(jnp.sum(total, axis=1, keepdims=True) * (1.0 / width) + EPS)
        inv_ref[pl.ds(r0, ROWS), :] = jnp.broadcast_to(inv, (ROWS, LANES))
        for b in range(blocks):
            lanes = slice(b * LANES, (b + 1) * LANES)
            normed = acc[b] * inv
            norm_ref[pl.ds(r0, ROWS), lanes] = normed
            gated = normed * gain_ref[:, lanes]
            act_ref[pl.ds(r0, ROWS), lanes] = (gated * jax.nn.sigmoid(gated)).astype(BF)
        return carry

    lax.fori_loop(0, length // ROWS, step, 0)


def product_kernel(mine_ref, got_ref, act_ref, act2_ref, out_ref):
    rows = mine_ref.shape[0]
    part = 128

    def step(i, carry):
        at = pl.ds(pl.multiple_of(i * part, part), part)
        total = jnp.dot(mine_ref[at, :], act_ref[...], preferred_element_type=F32)
        total = total + jnp.dot(got_ref[at, :], act2_ref[...], preferred_element_type=F32)
        out_ref[at, :] = total.astype(BF)
        return carry

    lax.fori_loop(0, rows // part, step, 0)


def norm_kernel(cot_ref, proj_ref, act_ref, norm_ref, inv_ref, gain_ref, out_ref, gm_ref, first_ref, last_ref, gg_ref):
    length, width = norm_ref.shape
    part = 64
    blocks = width // LANES
    nt = (((1,), (1,)), ((), ()))

    def step(i, carry):
        at = pl.ds(pl.multiple_of(i * part, part), part)
        out_ref[at, :] = lax.dot_general(act_ref[at, :], proj_ref[...], nt, preferred_element_type=F32).astype(BF)
        gm_ref[at, :] = jnp.dot(cot_ref[at, :], proj_ref[...], preferred_element_type=F32)
        return carry

    lax.fori_loop(0, length // part, step, 0)
    gg_ref[...] = jnp.zeros(gg_ref.shape, F32)

    def back(i, carry):
        at = pl.ds(pl.multiple_of(i * ROWS, ROWS), ROWS)
        sum_a = jnp.zeros((ROWS, LANES), F32)
        sum_b = jnp.zeros((ROWS, LANES), F32)
        kept = []
        for b in range(blocks):
            lanes = slice(b * LANES, (b + 1) * LANES)
            gain = gain_ref[:, lanes]
            normed = norm_ref[at, lanes]
            gated = normed * gain
            sigma = jax.nn.sigmoid(gated)
            gg = gm_ref[at, lanes] * sigma * (1.0 + gated * (1.0 - sigma))
            both = gg * normed
            rows8 = both[0:8]
            for r in range(8, ROWS, 8):
                rows8 = rows8 + both[r : r + 8]
            gg_ref[:, lanes] = gg_ref[:, lanes] + rows8
            gn = gg * gain
            sum_a = sum_a + gn
            sum_b = sum_b + gn * normed
            kept.append(gn)
        mean_a = jnp.sum(sum_a, axis=1, keepdims=True) * (1.0 / width)
        mean_b = jnp.sum(sum_b, axis=1, keepdims=True) * (1.0 / width)
        inv = inv_ref[at, :]
        for b in range(blocks):
            lanes = slice(b * LANES, (b + 1) * LANES)
            gm_ref[at, lanes] = inv * (kept[b] - mean_a - norm_ref[at, lanes] * mean_b)
        return carry

    lax.fori_loop(0, length // ROWS, back, 0)
    first_ref[...] = gm_ref[0:HALO, :]
    last_ref[...] = gm_ref[length - HALO : length, :]


def backward_kernel(
    own_rows, cols, core_ref, gm_ref, bef_ref, aft_ref, seg_ref, hid_ref, kern_ref, gg_ref, gh_ref, mine_ref, other_ref, win, kacc
):
    taps, width = kern_ref.shape
    length = hid_ref.shape[0]
    blocks = width // LANES
    group = 4
    spread(win, bef_ref, gm_ref, aft_ref)
    kacc[...] = jnp.zeros(kacc.shape, F32)

    def step(i, carry):
        r0 = pl.multiple_of(i * ROWS, ROWS)
        centre = seg_ref[pl.ds(r0 + HALO, ROWS), :]
        for g in range(blocks // group):
            own = range(g * group, (g + 1) * group)
            acc = {b: jnp.zeros((ROWS, LANES), F32) for b in own}
            hid = {b: hid_ref[pl.ds(r0, ROWS), b * LANES : (b + 1) * LANES].astype(F32) for b in own}
            for k in range(taps):
                same = seg_ref[pl.ds(r0 + taps - k, ROWS), :] == centre
                for b in own:
                    lanes = slice(b * LANES, (b + 1) * LANES)
                    grad = jnp.where(same, win[b, pl.ds(r0 + taps - k, ROWS), :], 0.0)
                    acc[b] = acc[b] + grad * kern_ref[k : k + 1, lanes]
                    prod = grad * hid[b]
                    rows8 = prod[0:8]
                    for r in range(8, ROWS, 8):
                        rows8 = rows8 + prod[r : r + 8]
                    kacc[k, :, lanes] = kacc[k, :, lanes] + rows8
            for b in own:
                gh_ref[pl.ds(r0, ROWS), b * LANES : (b + 1) * LANES] = acc[b].astype(BF)
        return carry

    lax.fori_loop(0, length // ROWS, step, 0)
    for b in range(blocks):
        lanes = slice(b * LANES, (b + 1) * LANES)
        rows = [jnp.sum(kacc[k, :, lanes], axis=0, keepdims=True) for k in range(taps)]
        rows.append(jnp.sum(gg_ref[:, lanes], axis=0, keepdims=True))
        rows.append(jnp.zeros((LANES - taps - 1, LANES), F32))
        deal(core_ref[0], b, jnp.concatenate(rows, axis=0).T, own_rows, cols, mine_ref, other_ref)


def join_kernel(landed_ref, t0_ref, t1_ref, t2_ref, t3_ref, out_ref):
    count, rows, width = landed_ref.shape

    def step(i, carry):
        at = pl.ds(pl.multiple_of(i * ROWS, ROWS), ROWS)
        total = landed_ref[0, at, :].astype(F32)
        for j in range(1, count):
            total = total + landed_ref[j, at, :].astype(F32)
        out_ref[at, :width] = total.astype(BF)
        out_ref[at, width:] = ((t0_ref[at, :] + t1_ref[at, :]) + (t2_ref[at, :] + t3_ref[at, :])).astype(BF)
        return carry

    lax.fori_loop(0, rows // ROWS, step, 0)


def final_kernel(factor, taps, a_ref, b_ref, c_ref, weight_ref, small_ref, gain_ref):
    low, high = jnp.minimum(a_ref[...], b_ref[...]), jnp.maximum(a_ref[...], b_ref[...])
    middle = jnp.maximum(low, jnp.minimum(high, c_ref[...]))
    total = ((jnp.minimum(low, c_ref[...]) + jnp.maximum(high, c_ref[...])) + middle) * factor
    width = weight_ref.shape[1]
    weight_ref[...] = total[:, :width]
    small_ref[...] = total[:, width : width + taps]
    gain_ref[...] = total[:, width:].T[taps : taps + 1, :]


SEQ = ("y", "x", "core")


def shifted(value, steps):
    count = lax.axis_size("y") * lax.axis_size("x") * lax.axis_size("core")
    first, last = max(0, -steps), min(count, count - steps)
    return lax.ppermute(value, SEQ, [(i, i + steps) for i in range(first, last)])


def over_groups(value):
    count = lax.axis_size("dp")

    def partner(mask):
        return lax.ppermute(value, "dp", [(i, i ^ mask) for i in range(count)])

    one, two, three = partner(1), partner(2), partner(3)
    value = (value + one) + (two + three)

    def ahead(by):
        return lax.ppermute(value, "dp", [(i, (i + by) % count) for i in range(count)])

    return value, ahead(4), ahead(count - 4)


def inner(hidden, segment_ids, kernel, norm_gain, projection, cotangent):
    frames = hidden[0]
    length, width = frames.shape
    taps = kernel.shape[0]
    cot = cotangent[0]
    ny, nx = lax.axis_size("y"), lax.axis_size("x")
    core = lax.axis_index("core")
    index = (lax.axis_index("y") * nx + lax.axis_index("x")) * 2 + core
    seg_row = jnp.pad(segment_ids[0], HALO, constant_values=-1)
    seg = lax.dynamic_slice_in_dim(seg_row, index * length, length + 2 * HALO)
    seg = jnp.broadcast_to(seg[:, None], (length + 2 * HALO, LANES))
    gain = norm_gain[None, :]
    swap = [(0, 1), (1, 0)]
    own = width // (ny * nx * 2)
    place = core[None]
    big = 2 * length * width * width
    vec = length * width * taps

    before = shifted(frames[length - HALO :], 1)
    after = shifted(frames[:HALO], -1)
    half = jax.ShapeDtypeStruct((width // 2, length), BF)
    mine, other = call(partial(split_kernel, own, nx), (half, half), smem=(0,), moved=4 * length * width)(place, cot)
    got = lax.ppermute(other, "core", swap)

    rows_win = length + 2 * HALO
    window = pltpu.VMEM((width // LANES, rows_win, LANES), F32)
    act, normed, inv = call(
        forward_kernel,
        (
            jax.ShapeDtypeStruct((length, width), BF),
            jax.ShapeDtypeStruct((length, width), F32),
            jax.ShapeDtypeStruct((length, LANES), F32),
        ),
        [window],
        flops=3 * vec,
        moved=8 * length * width,
        trans=2 * length * width,
    )(frames, before, after, seg, kernel, gain)
    act2 = lax.ppermute(act, "core", swap)
    weight = call(
        product_kernel,
        jax.ShapeDtypeStruct((width // 2, width), BF),
        flops=big,
        moved=2 * (width * width + 3 * length * width),
    )(mine, got, act, act2)
    landed = lax.all_to_all(weight.reshape(nx, ny * own, width), "x", split_axis=0, concat_axis=0, tiled=True)

    edge = jax.ShapeDtypeStruct((HALO, width), F32)
    conv_out, grad_mixed, first, last, gain_part = call(
        norm_kernel,
        (
            jax.ShapeDtypeStruct((length, width), BF),
            jax.ShapeDtypeStruct((length, width), F32),
            edge,
            edge,
            jax.ShapeDtypeStruct((8, width), F32),
        ),
        flops=2 * big,
        moved=16 * length * width,
        trans=2 * length * width,
    )(cot, projection, act, normed, inv, gain)
    gm_before = shifted(last, 1)
    gm_after = shifted(first, -1)
    dealt = jax.ShapeDtypeStruct((width // 2, LANES), F32)
    grad_hidden, small, small_other = call(
        partial(backward_kernel, own, nx),
        (jax.ShapeDtypeStruct((length, width), BF), dealt, dealt),
        [window, pltpu.VMEM((taps, 8, width), F32)],
        flops=5 * vec,
        moved=12 * length * width,
        smem=(0,),
    )(place, grad_mixed, gm_before, gm_after, seg, frames, kernel, gain_part)
    small = (small + lax.ppermute(small_other, "core", swap)).reshape(nx, ny, own, LANES)
    column = lax.axis_index("x")
    pieces = [lax.dynamic_index_in_dim(small, column ^ m, 0, keepdims=False) for m in range(nx)]
    for m in range(1, nx):
        pieces[m] = lax.ppermute(pieces[m], "x", [(i, i ^ m) for i in range(nx)])
    pieces = [piece.reshape(ny * own, LANES) for piece in pieces]

    weight = call(
        join_kernel,
        jax.ShapeDtypeStruct((ny * own, width + LANES), BF),
        moved=12 * ny * own * width,
    )(landed, *pieces).reshape(ny, own, width + LANES)
    landed = lax.all_to_all(weight, "y", split_axis=0, concat_axis=0, tiled=True)
    share = jnp.sum(landed.astype(F32), axis=0)
    factor = 1.0 / math.sqrt(length * ny * nx * 2 * lax.axis_size("dp"))
    grad_weight, grad_kernel, grad_gain = call(
        partial(final_kernel, factor, taps),
        (
            jax.ShapeDtypeStruct((own, width), F32),
            jax.ShapeDtypeStruct((own, taps), F32),
            jax.ShapeDtypeStruct((1, own), F32),
        ),
        moved=16 * own * width,
    )(*over_groups(share))
    return conv_out[None], grad_hidden[None], grad_weight, grad_kernel, grad_gain[0]


def solution(mesh):
    dp, seq = mesh.devices.shape
    fine = Mesh(mesh.devices.reshape(dp, 8, seq // 16, 2), ("dp",) + SEQ)
    rows = P("dp", SEQ, None)
    in_specs = (rows, P("dp", None), P(), P(), P(), rows)
    out_specs = (rows, rows, P(SEQ, None), P(SEQ, None), P(SEQ))
    return jax.shard_map(inner, mesh=fine, in_specs=in_specs, out_specs=out_specs, check_vma=False)
```

```python
import math
from functools import partial

import jax
import jax.numpy as jnp
from jax import lax
from jax.experimental import pallas as pl
from jax.experimental.pallas import tpu as pltpu
from jax.sharding import Mesh
from jax.sharding import PartitionSpec as P


EPS = 1e-05
LANES = 128
HALO = 16
ROWS = 32
BF = jnp.bfloat16
F32 = jnp.float32


def call(kernel, outs, scratch=(), flops=0, moved=0, trans=0, hbm=(), far=0, limit=9):
    def run(*args):
        specs = [
            pl.BlockSpec(memory_space=pltpu.HBM if i in hbm else pltpu.VMEM)
            for i in range(len(args))
        ]
        args = [
            pltpu.with_memory_space_constraint(arg, pltpu.HBM) if i in hbm else arg
            for i, arg in enumerate(args)
        ]
        return pl.pallas_call(
            kernel,
            out_shape=outs,
            in_specs=specs,
            out_specs=jax.tree.unflatten(
                jax.tree.structure(outs),
                [
                    pl.BlockSpec(memory_space=pltpu.HBM if i < far else pltpu.VMEM)
                    for i in range(len(jax.tree.leaves(outs)))
                ],
            ),
            scratch_shapes=list(scratch),
            compiler_params=pltpu.CompilerParams(vmem_limit_bytes=limit * 1024 * 1024),
            cost_estimate=pl.CostEstimate(flops=flops, bytes_accessed=moved, transcendentals=trans),
        )(*args)

    return run


def deal(core, b, turned, own, mine_ref, other_ref):
    pairs = LANES // (2 * own)
    for j in range(pairs):
        even = turned[2 * own * j : 2 * own * j + own]
        odd = turned[2 * own * j + own : 2 * own * j + 2 * own]
        at = (b * pairs + j) * own
        mine_ref[at : at + own, :] = jnp.where(core == 0, even, odd)
        other_ref[at : at + own, :] = jnp.where(core == 0, odd, even)


def place_of(axes):
    index = lax.axis_index(axes[0])
    for axis in axes[1:]:
        index = index * lax.axis_size(axis) + lax.axis_index(axis)
    return index


def first_kernel(
    own, ids_hbm, cot_hbm, hid_hbm, proj_hbm, kern_hbm, gain_hbm,
    mine_ref, other_ref, seg_ref, mid_ref, ga_ref, proj_ref, kern_ref, gain_ref,
    ids_ref, cot_ref, hid_ref, sems,
):
    pairs = (
        (cot_hbm, cot_ref), (ids_hbm, ids_ref), (hid_hbm, hid_ref),
        (kern_hbm, kern_ref), (gain_hbm, gain_ref), (proj_hbm, proj_ref),
    )
    copies = [pltpu.make_async_copy(src, dst, sems.at[i]) for i, (src, dst) in enumerate(pairs)]
    for copy in copies:
        copy.start()
    copies[0].wait()
    core = lax.axis_index("core")
    length, width = cot_ref.shape
    for b in range(width // LANES):
        turned = cot_ref[:, b * LANES : (b + 1) * LANES].T
        deal(core, b, turned, own, mine_ref, other_ref)
    copies[1].wait()
    index = place_of(SEQ)
    lines = length // LANES
    last = ids_ref.shape[0] - 1

    def column(line, outside):
        row = ids_ref[pl.ds(jnp.clip(line, 0, last), 1), :].astype(F32)
        square = jnp.broadcast_to(row, (LANES, LANES)).T
        return jnp.where(outside, -1.0, square)

    head = column(lines * index - 1, index == 0)
    seg_ref[0:HALO, :] = head[LANES - HALO :]
    for j in range(lines):
        seg_ref[HALO + j * LANES : HALO + (j + 1) * LANES, :] = column(lines * index + j, False)
    tail = column(lines * index + lines, lines * index + lines > last)
    seg_ref[HALO + length : 2 * HALO + length, :] = tail[:HALO]
    copies[2].wait()
    for b in range(width // LANES):
        mid_ref[b] = hid_ref[:, b * LANES : (b + 1) * LANES].astype(F32)
    for copy in copies[3:]:
        copy.wait()
    part = 64

    def step(i, carry):
        at = pl.ds(pl.multiple_of(i * part, part), part)
        ga_ref[at, :] = jnp.dot(cot_ref[at, :], proj_ref[...], preferred_element_type=F32)
        return carry

    lax.fori_loop(0, length // part, step, 0)


def edges_in(dst, before, after):
    blocks, rows = dst.shape[0], dst.shape[1]
    for b in range(blocks):
        lanes = slice(b * LANES, (b + 1) * LANES)
        dst[b, 0:HALO, :] = before[:, lanes].astype(F32)
        dst[b, rows - HALO : rows, :] = after[:, lanes].astype(F32)


def forward_kernel(mid_ref, bef_ref, aft_ref, seg_ref, kern_ref, gain_ref, act_ref, norm_ref, inv_ref, win):
    taps, width = kern_ref.shape
    length = act_ref.shape[0]
    blocks = width // LANES
    edges_in(win, bef_ref, aft_ref)
    for b in range(blocks):
        win[b, HALO : HALO + length, :] = mid_ref[b]

    def step(i, carry):
        r0 = pl.multiple_of(i * ROWS, ROWS)
        centre = seg_ref[pl.ds(r0 + HALO, ROWS), :]
        acc = [jnp.zeros((ROWS, LANES), F32) for _ in range(blocks)]
        for k in range(taps):
            same = seg_ref[pl.ds(r0 + k + 1, ROWS), :] == centre
            for b in range(blocks):
                w = kern_ref[k : k + 1, b * LANES : (b + 1) * LANES]
                term = win[b, pl.ds(r0 + k + 1, ROWS), :] * w
                acc[b] = acc[b] + jnp.where(same, term, 0.0)
        total = acc[0]
        for b in range(1, blocks):
            total = total + acc[b]
        mean = jnp.sum(total, axis=1, keepdims=True) * (1.0 / width)
        acc = [a - mean for a in acc]
        total = acc[0] * acc[0]
        for b in range(1, blocks):
            total = total + acc[b] * acc[b]
        inv = lax.rsqrt(jnp.sum(total, axis=1, keepdims=True) * (1.0 / width) + EPS)
        inv_ref[pl.ds(r0, ROWS), :] = jnp.broadcast_to(inv, (ROWS, LANES))
        for b in range(blocks):
            lanes = slice(b * LANES, (b + 1) * LANES)
            normed = acc[b] * inv
            norm_ref[pl.ds(r0, ROWS), lanes] = normed
            gated = normed * gain_ref[:, lanes]
            act_ref[pl.ds(r0, ROWS), lanes] = (gated * jax.nn.sigmoid(gated)).astype(BF)
        return carry

    lax.fori_loop(0, length // ROWS, step, 0)


def product_kernel(mine_ref, got_ref, act_ref, act2_ref, small_ref, small2_ref, out_ref):
    rows = mine_ref.shape[0]
    width = act_ref.shape[1]
    part = 128

    def step(i, carry):
        at = pl.ds(pl.multiple_of(i * part, part), part)
        total = jnp.dot(mine_ref[at, :], act_ref[...], preferred_element_type=F32)
        total = total + jnp.dot(got_ref[at, :], act2_ref[...], preferred_element_type=F32)
        out_ref[at, :width] = total.astype(BF)
        out_ref[at, width:] = (small_ref[at, :] + small2_ref[at, :]).astype(BF)
        return carry

    lax.fori_loop(0, rows // part, step, 0)


def taps_kernel(
    own, ga_ref, norm_ref, inv_ref, gain_ref, seg_ref, win,
    gm_hbm, first_hbm, last_hbm, mine_ref, other_ref, kacc, gg_ref, gm_ref, sems,
):
    length, width = norm_ref.shape
    taps = kacc.shape[0]
    blocks = width // LANES
    group = 4
    gg_ref[...] = jnp.zeros(gg_ref.shape, F32)
    kacc[...] = jnp.zeros(kacc.shape, F32)

    def rows_of(value):
        rows8 = value[0:8]
        for r in range(8, ROWS, 8):
            rows8 = rows8 + value[r : r + 8]
        return rows8

    def step(i, carry):
        r0 = pl.multiple_of(i * ROWS, ROWS)
        at = pl.ds(r0, ROWS)
        sum_a = jnp.zeros((ROWS, LANES), F32)
        sum_b = jnp.zeros((ROWS, LANES), F32)
        for b in range(blocks):
            lanes = slice(b * LANES, (b + 1) * LANES)
            gain = gain_ref[:, lanes]
            normed = norm_ref[at, lanes]
            gated = normed * gain
            sigma = jax.nn.sigmoid(gated)
            gg = ga_ref[at, lanes] * sigma * (1.0 + gated * (1.0 - sigma))
            gg_ref[:, lanes] = gg_ref[:, lanes] + rows_of(gg * normed)
            gn = gg * gain
            sum_a = sum_a + gn
            sum_b = sum_b + gn * normed
            gm_ref[at, lanes] = gn
        mean_a = jnp.sum(sum_a, axis=1, keepdims=True) * (1.0 / width)
        mean_b = jnp.sum(sum_b, axis=1, keepdims=True) * (1.0 / width)
        inv = inv_ref[at, :]
        centre = seg_ref[pl.ds(r0 + HALO, ROWS), :]
        for g in range(blocks // group):
            grads = {}
            for b in range(g * group, (g + 1) * group):
                lanes = slice(b * LANES, (b + 1) * LANES)
                grads[b] = inv * (gm_ref[at, lanes] - mean_a - norm_ref[at, lanes] * mean_b)
                gm_ref[at, lanes] = grads[b]
            for k in range(taps):
                same = seg_ref[pl.ds(r0 + k + 1, ROWS), :] == centre
                for b, grad in grads.items():
                    lanes = slice(b * LANES, (b + 1) * LANES)
                    prod = jnp.where(same, win[b, pl.ds(r0 + k + 1, ROWS), :], 0.0) * grad
                    kacc[k, :, lanes] = kacc[k, :, lanes] + rows_of(prod)
        pltpu.make_async_copy(gm_ref.at[at], gm_hbm.at[at], sems.at[i]).start()
        return carry

    count = length // ROWS
    lax.fori_loop(0, count, step, 0)
    ends = (
        pltpu.make_async_copy(gm_ref.at[0:HALO], first_hbm, sems.at[count]),
        pltpu.make_async_copy(gm_ref.at[length - HALO : length], last_hbm, sems.at[count + 1]),
    )
    for copy in ends:
        copy.start()
    core = lax.axis_index("core")
    for b in range(blocks):
        lanes = slice(b * LANES, (b + 1) * LANES)
        rows = [jnp.sum(kacc[k, :, lanes], axis=0, keepdims=True) for k in range(taps)]
        rows.append(jnp.sum(gg_ref[:, lanes], axis=0, keepdims=True))
        rows.append(jnp.zeros((LANES - taps - 1, LANES), F32))
        deal(core, b, jnp.concatenate(rows, axis=0).T, own, mine_ref, other_ref)
    for i in range(count):
        at = pl.ds(i * ROWS, ROWS)
        pltpu.make_async_copy(gm_ref.at[at], gm_hbm.at[at], sems.at[i]).wait()
    for copy in ends:
        copy.wait()


def back_kernel(act_ref, proj_ref, gm_ref, bef_ref, aft_ref, seg_ref, kern_ref, out_ref, gh_ref, win):
    taps, width = kern_ref.shape
    length = act_ref.shape[0]
    blocks = width // LANES
    part = 64
    nt = (((1,), (1,)), ((), ()))
    edges_in(win, bef_ref, aft_ref)
    for b in range(blocks):
        win[b, HALO : HALO + length, :] = gm_ref[:, b * LANES : (b + 1) * LANES]

    def multiply(i, carry):
        at = pl.ds(pl.multiple_of(i * part, part), part)
        out_ref[at, :] = lax.dot_general(act_ref[at, :], proj_ref[...], nt, preferred_element_type=F32).astype(BF)
        return carry

    lax.fori_loop(0, length // part, multiply, 0)

    def step(i, carry):
        r0 = pl.multiple_of(i * ROWS, ROWS)
        centre = seg_ref[pl.ds(r0 + HALO, ROWS), :]
        acc = [jnp.zeros((ROWS, LANES), F32) for _ in range(blocks)]
        for k in range(taps):
            same = seg_ref[pl.ds(r0 + taps - k, ROWS), :] == centre
            for b in range(blocks):
                w = kern_ref[k : k + 1, b * LANES : (b + 1) * LANES]
                term = win[b, pl.ds(r0 + taps - k, ROWS), :] * w
                acc[b] = acc[b] + jnp.where(same, term, 0.0)
        for b in range(blocks):
            gh_ref[pl.ds(r0, ROWS), b * LANES : (b + 1) * LANES] = acc[b].astype(BF)
        return carry

    lax.fori_loop(0, length // ROWS, step, 0)


def add_kernel(landed_ref, out_ref):
    count = landed_ref.shape[0]
    for b in range(out_ref.shape[1] // LANES):
        lanes = slice(b * LANES, (b + 1) * LANES)
        total = landed_ref[0, :, lanes].astype(F32)
        for j in range(1, count):
            total = total + landed_ref[j, :, lanes].astype(F32)
        out_ref[:, lanes] = total


def final_kernel(factor, taps, all_ref, weight_ref, small_ref, gain_ref):
    total = all_ref[0]
    for j in range(1, all_ref.shape[0]):
        total = total + all_ref[j]
    total = total * factor
    width = weight_ref.shape[1]
    weight_ref[...] = total[:, :width]
    small_ref[...] = total[:, width : width + taps]
    gain_ref[...] = total[:, width:].T[taps : taps + 1, :]


SEQ = ("y", "x", "core")


def shifted(value, steps):
    count = lax.axis_size("y") * lax.axis_size("x") * lax.axis_size("core")
    first, last = max(0, -steps), min(count, count - steps)
    return lax.ppermute(value, SEQ, [(i, i + steps) for i in range(first, last)])


def inner(hidden, segment_ids, kernel, norm_gain, projection, cotangent):
    frames = hidden[0]
    length, width = frames.shape
    taps = kernel.shape[0]
    cot = cotangent[0]
    ny, nx = lax.axis_size("y"), lax.axis_size("x")
    own = width // (ny * nx * 2)
    swap = [(0, 1), (1, 0)]
    big = 2 * length * width * width
    vec = length * width * taps
    shape = jax.ShapeDtypeStruct
    rows_win = length + 2 * HALO
    window = (width // LANES, rows_win, LANES)

    before = shifted(frames[length - HALO :], 1)
    after = shifted(frames[:HALO], -1)
    half = shape((width // 2, length), BF)
    ids = segment_ids.reshape(-1, LANES)
    mine, other, seg, mid, grad_act, proj, kern, gain = call(
        partial(first_kernel, own),
        (
            half,
            half,
            shape((rows_win, LANES), F32),
            shape((width // LANES, length, LANES), F32),
            shape((length, width), F32),
            shape((width, width), BF),
            shape((taps, width), F32),
            shape((1, width), F32),
        ),
        [
            pltpu.VMEM(ids.shape, ids.dtype),
            pltpu.VMEM((length, width), BF),
            pltpu.VMEM((length, width), BF),
            pltpu.SemaphoreType.DMA((6,)),
        ],
        flops=big,
        moved=12 * length * width,
        hbm=range(6),
    )(ids, cot, frames, projection, kernel, norm_gain[None, :])
    got = lax.ppermute(other, "core", swap)
    act, normed, inv, win = call(
        forward_kernel,
        (
            shape((length, width), BF),
            shape((length, width), F32),
            shape((length, LANES), F32),
            shape(window, F32),
        ),
        flops=3 * vec,
        moved=8 * length * width,
        trans=2 * length * width,
    )(mid, before, after, seg, kern, gain)
    act2 = lax.ppermute(act, "core", swap)
    far_edge = pltpu.HBM((HALO, width), F32)
    dealt = shape((width // 2, LANES), F32)
    grad_mixed, first, last, small, small_other = call(
        partial(taps_kernel, own),
        (pltpu.HBM((length, width), F32), far_edge, far_edge, dealt, dealt),
        [
            pltpu.VMEM((taps, 8, width), F32),
            pltpu.VMEM((8, width), F32),
            pltpu.VMEM((length, width), F32),
            pltpu.SemaphoreType.DMA((length // ROWS + 2,)),
        ],
        far=3,
        flops=3 * vec,
        moved=16 * length * width,
        trans=2 * length * width,
    )(grad_act, normed, inv, gain, seg, win)
    small2 = lax.ppermute(small_other, "core", swap)
    weight = call(
        product_kernel,
        shape((width // 2, width + LANES), BF),
        flops=big,
        moved=2 * (width * width + 3 * length * width),
    )(mine, got, act, act2, small, small2)
    landed = lax.all_to_all(
        weight.reshape(ny * nx, own, width + LANES), ("y", "x"), split_axis=0, concat_axis=0, tiled=True
    )
    gm_before = shifted(last, 1)
    gm_after = shifted(first, -1)
    conv_out, grad_hidden = call(
        back_kernel,
        (shape((length, width), BF), shape((length, width), BF)),
        [pltpu.VMEM(window, F32)],
        flops=3 * vec + big,
        moved=12 * length * width,
    )(act, proj, grad_mixed, gm_before, gm_after, seg, kern)
    share = call(add_kernel, shape((own, width + LANES), F32), moved=80 * own * width)(landed)
    everyone = lax.all_gather(share, "dp")
    factor = 1.0 / math.sqrt(length * ny * nx * 2 * lax.axis_size("dp"))
    grad_weight, grad_kernel, grad_gain = call(
        partial(final_kernel, factor, taps),
        (shape((own, width), F32), shape((own, taps), F32), shape((1, own), F32)),
        moved=64 * own * width,
    )(everyone)
    return conv_out[None], grad_hidden[None], grad_weight, grad_kernel, grad_gain[0]


def solution(mesh):
    dp, seq = mesh.devices.shape
    fine = Mesh(mesh.devices.reshape(dp, 8, seq // 16, 2), ("dp",) + SEQ)
    rows = P("dp", SEQ, None)
    in_specs = (rows, P("dp", None), P(), P(), P(), rows)
    out_specs = (rows, rows, P(SEQ, None), P(SEQ, None), P(SEQ))
    return jax.shard_map(inner, mesh=fine, in_specs=in_specs, out_specs=out_specs, check_vma=False)
```

```python
import math
from functools import partial

import jax
import jax.numpy as jnp
from jax import lax
from jax.experimental import pallas as pl
from jax.experimental.pallas import tpu as pltpu
from jax.sharding import Mesh
from jax.sharding import PartitionSpec as P


EPS = 1e-05
LANES = 128
NEAR = 16
WIDE = 32
ROWS = 32
BF = jnp.bfloat16
F32 = jnp.float32


def call(kernel, outs, scratch=(), flops=0, moved=0, trans=0, hbm=(), far=0, limit=9):
    def run(*args):
        specs = [
            pl.BlockSpec(memory_space=pltpu.HBM if i in hbm else pltpu.VMEM)
            for i in range(len(args))
        ]
        args = [
            pltpu.with_memory_space_constraint(arg, pltpu.HBM) if i in hbm else arg
            for i, arg in enumerate(args)
        ]
        return pl.pallas_call(
            kernel,
            out_shape=outs,
            in_specs=specs,
            out_specs=jax.tree.unflatten(
                jax.tree.structure(outs),
                [
                    pl.BlockSpec(memory_space=pltpu.HBM if i < far else pltpu.VMEM)
                    for i in range(len(jax.tree.leaves(outs)))
                ],
            ),
            scratch_shapes=list(scratch),
            compiler_params=pltpu.CompilerParams(vmem_limit_bytes=limit * 1024 * 1024),
            cost_estimate=pl.CostEstimate(flops=flops, bytes_accessed=moved, transcendentals=trans),
        )(*args)

    return run


def deal(core, at, even, odd, mine_ref, other_ref):
    mine_ref[at : at + even.shape[0], :] = jnp.where(core == 0, even, odd)
    other_ref[at : at + even.shape[0], :] = jnp.where(core == 0, odd, even)


def place_of(axes):
    index = lax.axis_index(axes[0])
    for axis in axes[1:]:
        index = index * lax.axis_size(axis) + lax.axis_index(axis)
    return index


def matmul_into(out_ref, pairs, transposed=False):
    part = 256
    dims = (((1,), (1,)), ((), ())) if transposed else (((1,), (0,)), ((), ()))
    for n in range(out_ref.shape[1] // part):
        at = slice(n * part, (n + 1) * part)
        total = None
        for left, right in pairs:
            term = lax.dot_general(
                left[...], right[at, :] if transposed else right[:, at], dims, preferred_element_type=F32
            )
            total = term if total is None else total + term
        out_ref[:, at] = total.astype(out_ref.dtype)


def ends_kernel(hid_hbm, cot_hbm, up_ref, down_ref, sems):
    length = hid_hbm.shape[0]
    pairs = (
        (hid_hbm.at[length - WIDE : length], up_ref.at[0:WIDE]),
        (cot_hbm.at[length - NEAR : length], up_ref.at[WIDE : WIDE + NEAR]),
        (hid_hbm.at[0:WIDE], down_ref.at[0:WIDE]),
        (cot_hbm.at[0:NEAR], down_ref.at[WIDE : WIDE + NEAR]),
    )
    copies = [pltpu.make_async_copy(src, dst, sems.at[i]) for i, (src, dst) in enumerate(pairs)]
    for copy in copies:
        copy.start()
    for copy in copies:
        copy.wait()


def first_kernel(
    own, ids_hbm, cot_hbm, hid_hbm, proj_hbm, kern_hbm, gain_hbm,
    mine_ref, other_ref, seg_ref, mid_ref, ga_ref, kern_ref, gain_ref,
    ids_ref, cot_ref, hid_ref, proj_ref, sems,
):
    pairs = (
        (cot_hbm, cot_ref), (ids_hbm, ids_ref), (hid_hbm, hid_ref),
        (kern_hbm, kern_ref), (gain_hbm, gain_ref), (proj_hbm, proj_ref),
    )
    copies = [pltpu.make_async_copy(src, dst, sems.at[i]) for i, (src, dst) in enumerate(pairs)]
    for copy in copies:
        copy.start()
    copies[0].wait()
    core = lax.axis_index("core")
    length, width = cot_ref.shape
    for b in range(width // LANES):
        turned = cot_ref[:, b * LANES : (b + 1) * LANES].T
        for j in range(LANES // (2 * own)):
            at = 2 * own * j
            even, odd = turned[at : at + own], turned[at + own : at + 2 * own]
            deal(core, (b * (LANES // (2 * own)) + j) * own, even, odd, mine_ref, other_ref)
    copies[1].wait()
    index = place_of(SEQ)
    lines = length // LANES
    last = ids_ref.shape[0] - 1

    def column(line, outside):
        row = ids_ref[pl.ds(jnp.clip(line, 0, last), 1), :].astype(F32)
        square = jnp.broadcast_to(row, (LANES, LANES)).T
        return jnp.where(outside, -1.0, square)

    head = column(lines * index - 1, index == 0)
    seg_ref[0:WIDE, :] = head[LANES - WIDE :]
    for j in range(lines):
        seg_ref[WIDE + j * LANES : WIDE + (j + 1) * LANES, :] = column(lines * index + j, False)
    tail = column(lines * index + lines, lines * index + lines > last)
    seg_ref[WIDE + length : 2 * WIDE + length, :] = tail[:WIDE]
    copies[2].wait()
    for b in range(width // LANES):
        mid_ref[b] = hid_ref[:, b * LANES : (b + 1) * LANES].astype(F32)
    for copy in copies[3:]:
        copy.wait()
    matmul_into(ga_ref, ((cot_ref, proj_ref),))


def convolved(win, wr, seg_ref, sr, kern_ref, rows):
    taps, width = kern_ref.shape
    blocks = width // LANES
    centre = seg_ref[pl.ds(sr + taps // 2, rows), :]
    acc = [jnp.zeros((rows, LANES), F32) for _ in range(blocks)]
    for k in range(taps):
        same = seg_ref[pl.ds(sr + k, rows), :] == centre
        for b in range(blocks):
            term = win[b, pl.ds(wr + k, rows), :] * kern_ref[k : k + 1, b * LANES : (b + 1) * LANES]
            acc[b] = acc[b] + jnp.where(same, term, 0.0)
    return acc


def mean_of(parts, width):
    total = parts[0]
    for part in parts[1:]:
        total = total + part
    return jnp.sum(total, axis=1, keepdims=True) * (1.0 / width)


def normalised(acc, width):
    mean = mean_of(acc, width)
    acc = [a - mean for a in acc]
    inv = lax.rsqrt(mean_of([a * a for a in acc], width) + EPS)
    return [a * inv for a in acc], inv


def gate_back(grad, normed, gain):
    gated = normed * gain
    sigma = jax.nn.sigmoid(gated)
    return grad * sigma * (1.0 + gated * (1.0 - sigma))


def forward_kernel(
    mid_ref, bef_ref, aft_ref, seg_ref, kern_ref, gain_ref, other_ref, pack_ref, norm_ref, inv_ref, win
):
    taps, width = kern_ref.shape
    length = norm_ref.shape[0]
    blocks = width // LANES
    for b in range(blocks):
        lanes = slice(b * LANES, (b + 1) * LANES)
        win[b, 0:WIDE, :] = bef_ref[0:WIDE, lanes].astype(F32)
        win[b, WIDE : WIDE + length, :] = mid_ref[b]
        win[b, WIDE + length :, :] = aft_ref[0:WIDE, lanes].astype(F32)
    for j in range(width // length):
        rows = other_ref.shape[0] * length // width
        pack_ref[length:, j * length : (j + 1) * length] = other_ref[j * rows : (j + 1) * rows, :]
    off = WIDE - taps // 2

    def step(i, carry):
        r0 = pl.multiple_of(i * ROWS, ROWS)
        normed, inv = normalised(convolved(win, r0 + off, seg_ref, r0 + off, kern_ref, ROWS), width)
        inv_ref[pl.ds(r0, ROWS), :] = jnp.broadcast_to(inv, (ROWS, LANES))
        for b in range(blocks):
            lanes = slice(b * LANES, (b + 1) * LANES)
            norm_ref[pl.ds(r0, ROWS), lanes] = normed[b]
            gated = normed[b] * gain_ref[:, lanes]
            pack_ref[pl.ds(r0, ROWS), lanes] = (gated * jax.nn.sigmoid(gated)).astype(BF)
        return carry

    lax.fori_loop(0, length // ROWS, step, 0)


def product_kernel(own, mine_ref, pack_ref, pack2_ref, small_ref, small2_ref, out_hbm, out_ref, sems):
    rows, length = mine_ref.shape
    width = pack_ref.shape[1]
    count = rows // own
    part = 256
    deep = rows * length // width
    got = [pack2_ref[length:, j * length : (j + 1) * length] for j in range(rows // deep)]
    got = jnp.concatenate(got, axis=0)
    copies = []

    def send(first, last):
        at = slice(first, last)
        copies.append(pltpu.make_async_copy(out_ref.at[:, at], out_hbm.at[:, at], sems.at[len(copies)]))
        copies[-1].start()

    line = width // LANES * own
    small = (small_ref[...] + small2_ref[...]).astype(BF)
    out_ref[:, line:, :] = small.reshape(count, own // 2, LANES)
    send(line, line + own // 2)
    for n in range(width // part):
        at = slice(n * part, (n + 1) * part)
        total = jnp.dot(mine_ref[...], pack_ref[0:length, at], preferred_element_type=F32)
        total = total + jnp.dot(got, pack2_ref[0:length, at], preferred_element_type=F32)
        total = total.astype(BF).reshape(count, own, part)
        for b in range(part // LANES):
            line = (n * (part // LANES) + b) * own
            out_ref[:, line : line + own, :] = total[:, :, b * LANES : (b + 1) * LANES]
        send(n * (part // LANES) * own, (n + 1) * (part // LANES) * own)
    for copy in copies:
        copy.wait()


def taps_kernel(
    own, ga_ref, norm_ref, inv_ref, gain_ref, seg_ref, win,
    gm_hbm, mine_ref, other_ref, kacc, gg_ref, gm_ref, sems,
):
    length, width = norm_ref.shape
    taps = kacc.shape[0]
    blocks = width // LANES
    group = 4
    off = WIDE - taps // 2
    gg_ref[...] = jnp.zeros(gg_ref.shape, F32)
    kacc[...] = jnp.zeros(kacc.shape, F32)

    def rows_of(value):
        rows8 = value[0:8]
        for r in range(8, ROWS, 8):
            rows8 = rows8 + value[r : r + 8]
        return rows8

    def step(i, carry):
        r0 = pl.multiple_of(i * ROWS, ROWS)
        at = pl.ds(r0, ROWS)
        sum_a = jnp.zeros((ROWS, LANES), F32)
        sum_b = jnp.zeros((ROWS, LANES), F32)
        for b in range(blocks):
            lanes = slice(b * LANES, (b + 1) * LANES)
            gain = gain_ref[:, lanes]
            normed = norm_ref[at, lanes]
            gg = gate_back(ga_ref[at, lanes], normed, gain)
            gg_ref[:, lanes] = gg_ref[:, lanes] + rows_of(gg * normed)
            gn = gg * gain
            sum_a = sum_a + gn
            sum_b = sum_b + gn * normed
            gm_ref[at, lanes] = gn
        mean_a = jnp.sum(sum_a, axis=1, keepdims=True) * (1.0 / width)
        mean_b = jnp.sum(sum_b, axis=1, keepdims=True) * (1.0 / width)
        inv = inv_ref[at, :]
        centre = seg_ref[pl.ds(r0 + WIDE, ROWS), :]
        for g in range(blocks // group):
            grads = {}
            for b in range(g * group, (g + 1) * group):
                lanes = slice(b * LANES, (b + 1) * LANES)
                grads[b] = inv * (gm_ref[at, lanes] - mean_a - norm_ref[at, lanes] * mean_b)
                gm_ref[at, lanes] = grads[b]
            for k in range(taps):
                same = seg_ref[pl.ds(r0 + off + k, ROWS), :] == centre
                for b, grad in grads.items():
                    lanes = slice(b * LANES, (b + 1) * LANES)
                    prod = jnp.where(same, win[b, pl.ds(r0 + off + k, ROWS), :], 0.0) * grad
                    kacc[k, :, lanes] = kacc[k, :, lanes] + rows_of(prod)
        pltpu.make_async_copy(gm_ref.at[at], gm_hbm.at[at], sems.at[i]).start()
        return carry

    count = length // ROWS
    lax.fori_loop(0, count, step, 0)
    core = lax.axis_index("core")
    half = own // 2
    upper = (lax.broadcasted_iota(jnp.int32, (taps + 1, LANES), 1) // half) % 2 == 1
    for b in range(blocks):
        lanes = slice(b * LANES, (b + 1) * LANES)
        rows = [jnp.sum(kacc[k, :, lanes], axis=0, keepdims=True) for k in range(taps)]
        rows.append(jnp.sum(gg_ref[:, lanes], axis=0, keepdims=True))
        rows = jnp.concatenate(rows, axis=0)
        pad = jnp.zeros((LANES - 2 * (taps + 1), LANES), F32)
        turned = jnp.concatenate([jnp.where(upper, 0.0, rows), jnp.where(upper, rows, 0.0), pad], axis=0).T
        for j in range(LANES // (2 * own)):
            at = 2 * own * j
            even = turned[at : at + half] + turned[at + half : at + own]
            odd = turned[at + own : at + own + half] + turned[at + own + half : at + 2 * own]
            deal(core, (b * (LANES // (2 * own)) + j) * half, even, odd, mine_ref, other_ref)
    for i in range(count):
        at = pl.ds(i * ROWS, ROWS)
        pltpu.make_async_copy(gm_ref.at[at], gm_hbm.at[at], sems.at[i]).wait()


def back_kernel(
    pack_ref, proj_ref, gm_ref, bef_ref, aft_ref, seg_ref, kern_ref, gain_ref, hid_hbm,
    out_ref, gh_ref, gwin, hwin, hid_ref, ga_ref, sems,
):
    taps, width = kern_ref.shape
    length = gh_ref.shape[0]
    blocks = width // LANES
    copies = (
        pltpu.make_async_copy(hid_hbm.at[0:WIDE], hid_ref.at[0], sems.at[0]),
        pltpu.make_async_copy(hid_hbm.at[length - WIDE : length], hid_ref.at[1], sems.at[1]),
    )
    for copy in copies:
        copy.start()
    matmul_into(out_ref, ((pack_ref.at[0:length], proj_ref),), transposed=True)
    matmul_into(ga_ref.at[0:NEAR], ((bef_ref.at[WIDE:], proj_ref),))
    matmul_into(ga_ref.at[NEAR:], ((aft_ref.at[WIDE:], proj_ref),))
    for copy in copies:
        copy.wait()
    for b in range(blocks):
        lanes = slice(b * LANES, (b + 1) * LANES)
        gwin[b, NEAR : NEAR + length, :] = gm_ref[:, lanes]
        hwin[b, 0:WIDE, :] = bef_ref[0:WIDE, lanes].astype(F32)
        hwin[b, WIDE : 2 * WIDE, :] = hid_ref[0, :, lanes].astype(F32)
        hwin[b, 2 * WIDE : 3 * WIDE, :] = hid_ref[1, :, lanes].astype(F32)
        hwin[b, 3 * WIDE :, :] = aft_ref[0:WIDE, lanes].astype(F32)
    reach = taps // 2
    sides = (
        (NEAR - reach, NEAR - reach, 0, 0),
        (3 * WIDE - reach, WIDE + length - reach, NEAR, NEAR + length),
    )
    for wr, sr, ar, to in sides:
        normed, inv = normalised(convolved(hwin, wr, seg_ref, sr, kern_ref, NEAR), width)
        grads = []
        for b in range(blocks):
            lanes = slice(b * LANES, (b + 1) * LANES)
            gain = gain_ref[:, lanes]
            grads.append(gate_back(ga_ref[ar : ar + NEAR, lanes], normed[b], gain) * gain)
        mean_a = mean_of(grads, width)
        mean_b = mean_of([g * n for g, n in zip(grads, normed)], width)
        for b in range(blocks):
            gwin[b, to : to + NEAR, :] = inv * (grads[b] - mean_a - normed[b] * mean_b)

    def step(i, carry):
        r0 = pl.multiple_of(i * ROWS, ROWS)
        centre = seg_ref[pl.ds(r0 + WIDE, ROWS), :]
        acc = [jnp.zeros((ROWS, LANES), F32) for _ in range(blocks)]
        for k in range(taps):
            line = NEAR + reach - k
            same = seg_ref[pl.ds(r0 + line + WIDE - NEAR, ROWS), :] == centre
            for b in range(blocks):
                w = kern_ref[k : k + 1, b * LANES : (b + 1) * LANES]
                term = gwin[b, pl.ds(r0 + line, ROWS), :] * w
                acc[b] = acc[b] + jnp.where(same, term, 0.0)
        for b in range(blocks):
            gh_ref[pl.ds(r0, ROWS), b * LANES : (b + 1) * LANES] = acc[b].astype(BF)
        return carry

    lax.fori_loop(0, length // ROWS, step, 0)


def add_kernel(landed_ref, out_ref):
    total = landed_ref[0].astype(F32)
    for j in range(1, landed_ref.shape[0]):
        total = total + landed_ref[j].astype(F32)
    out_ref[...] = total


def final_kernel(factor, taps, all_ref, weight_ref, small_ref, gain_ref):
    total = all_ref[0]
    for j in range(1, all_ref.shape[0]):
        total = total + all_ref[j]
    total = total * factor
    own, width = weight_ref.shape
    for b in range(width // LANES):
        weight_ref[:, b * LANES : (b + 1) * LANES] = total[b * own : (b + 1) * own, :]
    tail = total[width // LANES * own :, :]
    tail = jnp.concatenate([tail[:, : taps + 1], tail[:, taps + 1 : 2 * (taps + 1)]], axis=0)
    small_ref[...] = tail[:, :taps]
    wide = jnp.concatenate([tail, jnp.zeros((own, LANES - taps - 1), F32)], axis=1)
    gain_ref[...] = wide.T[taps : taps + 1, :]


SEQ = ("y", "x", "core")


def shifted(value, steps):
    count = lax.axis_size("y") * lax.axis_size("x") * lax.axis_size("core")
    first, last = max(0, -steps), min(count, count - steps)
    return lax.ppermute(value, SEQ, [(i, i + steps) for i in range(first, last)])


def inner(hidden, segment_ids, kernel, norm_gain, projection, cotangent):
    frames = hidden[0]
    length, width = frames.shape
    taps = kernel.shape[0]
    cot = cotangent[0]
    ny, nx = lax.axis_size("y"), lax.axis_size("x")
    own = width // (ny * nx * 2)
    swap = [(0, 1), (1, 0)]
    big = 2 * length * width * width
    vec = length * width * taps
    shape = jax.ShapeDtypeStruct
    rows_win = length + 2 * WIDE
    blocks = width // LANES
    window = (blocks, rows_win, LANES)
    lines = (blocks * own) + own // 2

    message = shape((WIDE + NEAR, width), BF)
    up, down = call(
        ends_kernel, (message, message), [pltpu.SemaphoreType.DMA((4,))], moved=512 * width, hbm=(0, 1)
    )(frames, cot)
    before = shifted(up, 1)
    after = shifted(down, -1)
    half = shape((width // 2, length), BF)
    ids = segment_ids.reshape(-1, LANES)
    mine, other, seg, mid, grad_act, kern, gain = call(
        partial(first_kernel, own),
        (
            half,
            half,
            shape((rows_win, LANES), F32),
            shape((blocks, length, LANES), F32),
            shape((length, width), F32),
            shape((taps, width), F32),
            shape((1, width), F32),
        ),
        [
            pltpu.VMEM(ids.shape, ids.dtype),
            pltpu.VMEM((length, width), BF),
            pltpu.VMEM((length, width), BF),
            pltpu.VMEM((width, width), BF),
            pltpu.SemaphoreType.DMA((6,)),
        ],
        flops=big,
        moved=12 * length * width,
        hbm=range(6),
    )(ids, cot, frames, projection, kernel, norm_gain[None, :])
    pack, normed, inv, win = call(
        forward_kernel,
        (
            shape((length + length // 2, width), BF),
            shape((length, width), F32),
            shape((length, LANES), F32),
            shape(window, F32),
        ),
        flops=3 * vec,
        moved=8 * length * width,
        trans=2 * length * width,
    )(mid, before, after, seg, kern, gain, other)
    pack2 = lax.ppermute(pack, "core", swap)
    dealt = shape((width // 4, LANES), F32)
    grad_mixed, small, small_other = call(
        partial(taps_kernel, own),
        (pltpu.HBM((length, width), F32), dealt, dealt),
        [
            pltpu.VMEM((taps, 8, width), F32),
            pltpu.VMEM((8, width), F32),
            pltpu.VMEM((length, width), F32),
            pltpu.SemaphoreType.DMA((length // ROWS,)),
        ],
        far=1,
        flops=3 * vec,
        moved=16 * length * width,
        trans=2 * length * width,
    )(grad_act, normed, inv, gain, seg, win)
    small2 = lax.ppermute(small_other, "core", swap)
    weight = call(
        partial(product_kernel, own),
        pltpu.HBM((ny * nx, lines, LANES), BF),
        [pltpu.VMEM((ny * nx, lines, LANES), BF), pltpu.SemaphoreType.DMA((width // 256 + 1,))],
        far=1,
        flops=big,
        moved=2 * (width * width + 3 * length * width),
    )(mine, pack, pack2, small, small2)
    landed = lax.all_to_all(weight, ("y", "x"), split_axis=0, concat_axis=0, tiled=True)
    conv_out, grad_hidden = call(
        back_kernel,
        (shape((length, width), BF), shape((length, width), BF)),
        [
            pltpu.VMEM((blocks, length + 2 * NEAR, LANES), F32),
            pltpu.VMEM((blocks, 4 * WIDE, LANES), F32),
            pltpu.VMEM((2, WIDE, width), BF),
            pltpu.VMEM((2 * NEAR, width), F32),
            pltpu.SemaphoreType.DMA((2,)),
        ],
        flops=3 * vec + big,
        moved=12 * length * width,
        hbm=(8,),
    )(pack, projection, grad_mixed, before, after, seg, kern, gain, frames)
    share = call(add_kernel, shape((lines, LANES), F32), moved=80 * own * width)(landed)
    everyone = lax.all_gather(share, "dp")
    factor = 1.0 / math.sqrt(length * ny * nx * 2 * lax.axis_size("dp"))
    grad_weight, grad_kernel, grad_gain = call(
        partial(final_kernel, factor, taps),
        (shape((own, width), F32), shape((own, taps), F32), shape((1, own), F32)),
        moved=64 * own * width,
    )(everyone)
    return conv_out[None], grad_hidden[None], grad_weight, grad_kernel, grad_gain[0]


def solution(mesh):
    dp, seq = mesh.devices.shape
    fine = Mesh(mesh.devices.reshape(dp, 8, seq // 16, 2), ("dp",) + SEQ)
    rows = P("dp", SEQ, None)
    in_specs = (rows, P("dp", None), P(), P(), P(), rows)
    out_specs = (rows, rows, P(SEQ, None), P(SEQ, None), P(SEQ))
    return jax.shard_map(inner, mesh=fine, in_specs=in_specs, out_specs=out_specs, check_vma=False)
```

```python
import math
from functools import partial

import jax
import jax.numpy as jnp
from jax import lax
from jax.experimental import pallas as pl
from jax.experimental.pallas import tpu as pltpu
from jax.sharding import Mesh
from jax.sharding import PartitionSpec as P


EPS = 1e-05
LANES = 128
NEAR = 16
WIDE = 32
ROWS = 32
BF = jnp.bfloat16
F32 = jnp.float32


def call(kernel, outs, scratch=(), flops=0, moved=0, trans=0, hbm=(), far=0, limit=9):
    def run(*args):
        specs = [
            pl.BlockSpec(memory_space=pltpu.HBM if i in hbm else pltpu.VMEM)
            for i in range(len(args))
        ]
        args = [
            pltpu.with_memory_space_constraint(arg, pltpu.HBM) if i in hbm else arg
            for i, arg in enumerate(args)
        ]
        return pl.pallas_call(
            kernel,
            out_shape=outs,
            in_specs=specs,
            out_specs=jax.tree.unflatten(
                jax.tree.structure(outs),
                [
                    pl.BlockSpec(memory_space=pltpu.HBM if i < far else pltpu.VMEM)
                    for i in range(len(jax.tree.leaves(outs)))
                ],
            ),
            scratch_shapes=list(scratch),
            compiler_params=pltpu.CompilerParams(vmem_limit_bytes=limit * 1024 * 1024),
            cost_estimate=pl.CostEstimate(flops=flops, bytes_accessed=moved, transcendentals=trans),
        )(*args)

    return run


def deal(core, at, even, odd, mine_ref, other_ref):
    mine_ref[at : at + even.shape[0], :] = jnp.where(core == 0, even, odd)
    other_ref[at : at + even.shape[0], :] = jnp.where(core == 0, odd, even)


def place_of(axes):
    index = lax.axis_index(axes[0])
    for axis in axes[1:]:
        index = index * lax.axis_size(axis) + lax.axis_index(axis)
    return index


def matmul_into(out_ref, pairs, transposed=False):
    part = 256
    dims = (((1,), (1,)), ((), ())) if transposed else (((1,), (0,)), ((), ()))
    for n in range(out_ref.shape[1] // part):
        at = slice(n * part, (n + 1) * part)
        total = None
        for left, right in pairs:
            term = lax.dot_general(
                left[...], right[at, :] if transposed else right[:, at], dims, preferred_element_type=F32
            )
            total = term if total is None else total + term
        out_ref[:, at] = total.astype(out_ref.dtype)


def ends_kernel(hid_hbm, cot_hbm, up_ref, down_ref, sems):
    length = hid_hbm.shape[0]
    pairs = (
        (hid_hbm.at[length - WIDE : length], up_ref.at[0:WIDE]),
        (cot_hbm.at[length - NEAR : length], up_ref.at[WIDE : WIDE + NEAR]),
        (hid_hbm.at[0:WIDE], down_ref.at[0:WIDE]),
        (cot_hbm.at[0:NEAR], down_ref.at[WIDE : WIDE + NEAR]),
    )
    copies = [pltpu.make_async_copy(src, dst, sems.at[i]) for i, (src, dst) in enumerate(pairs)]
    for copy in copies:
        copy.start()
    for copy in copies:
        copy.wait()


def first_kernel(
    own, ids_hbm, cot_hbm, hid_hbm, proj_hbm, kern_hbm, gain_hbm,
    mine_ref, other_ref, seg_ref, mid_ref, ga_ref, kern_ref, gain_ref,
    ids_ref, cot_ref, hid_ref, proj_ref, sems,
):
    pairs = (
        (cot_hbm, cot_ref), (ids_hbm, ids_ref), (hid_hbm, hid_ref),
        (kern_hbm, kern_ref), (gain_hbm, gain_ref), (proj_hbm, proj_ref),
    )
    copies = [pltpu.make_async_copy(src, dst, sems.at[i]) for i, (src, dst) in enumerate(pairs)]
    for copy in copies:
        copy.start()
    copies[0].wait()
    core = lax.axis_index("core")
    length, width = cot_ref.shape
    for b in range(width // LANES):
        turned = cot_ref[:, b * LANES : (b + 1) * LANES].T
        for j in range(LANES // (2 * own)):
            at = 2 * own * j
            even, odd = turned[at : at + own], turned[at + own : at + 2 * own]
            deal(core, (b * (LANES // (2 * own)) + j) * own, even, odd, mine_ref, other_ref)
    copies[1].wait()
    index = place_of(SEQ)
    lines = length // LANES
    last = ids_ref.shape[0] - 1

    def column(line, outside):
        row = ids_ref[pl.ds(jnp.clip(line, 0, last), 1), :].astype(F32)
        square = jnp.broadcast_to(row, (LANES, LANES)).T
        return jnp.where(outside, -1.0, square)

    head = column(lines * index - 1, index == 0)
    seg_ref[0:WIDE, :] = head[LANES - WIDE :]
    for j in range(lines):
        seg_ref[WIDE + j * LANES : WIDE + (j + 1) * LANES, :] = column(lines * index + j, False)
    tail = column(lines * index + lines, lines * index + lines > last)
    seg_ref[WIDE + length : 2 * WIDE + length, :] = tail[:WIDE]
    copies[2].wait()
    for b in range(width // LANES):
        mid_ref[b] = hid_ref[:, b * LANES : (b + 1) * LANES].astype(F32)
    for copy in copies[3:]:
        copy.wait()
    matmul_into(ga_ref, ((cot_ref, proj_ref),))


def convolved(win, wr, seg_ref, sr, kern_ref, rows):
    taps, width = kern_ref.shape
    blocks = width // LANES
    centre = seg_ref[pl.ds(sr + taps // 2, rows), :]
    acc = [jnp.zeros((rows, LANES), F32) for _ in range(blocks)]
    for k in range(taps):
        same = seg_ref[pl.ds(sr + k, rows), :] == centre
        for b in range(blocks):
            term = win[b, pl.ds(wr + k, rows), :] * kern_ref[k : k + 1, b * LANES : (b + 1) * LANES]
            acc[b] = acc[b] + jnp.where(same, term, 0.0)
    return acc


def mean_of(parts, width):
    total = parts[0]
    for part in parts[1:]:
        total = total + part
    return jnp.sum(total, axis=1, keepdims=True) * (1.0 / width)


def normalised(acc, width):
    mean = mean_of(acc, width)
    acc = [a - mean for a in acc]
    inv = lax.rsqrt(mean_of([a * a for a in acc], width) + EPS)
    return [a * inv for a in acc], inv


def gate_back(grad, normed, gain):
    gated = normed * gain
    sigma = jax.nn.sigmoid(gated)
    return grad * sigma * (1.0 + gated * (1.0 - sigma))


def forward_kernel(
    mid_ref, bef_ref, aft_ref, seg_ref, kern_ref, gain_ref, other_ref, pack_ref, norm_ref, inv_ref, win
):
    taps, width = kern_ref.shape
    length = norm_ref.shape[0]
    blocks = width // LANES
    for b in range(blocks):
        lanes = slice(b * LANES, (b + 1) * LANES)
        win[b, 0:WIDE, :] = bef_ref[0:WIDE, lanes].astype(F32)
        win[b, WIDE : WIDE + length, :] = mid_ref[b]
        win[b, WIDE + length :, :] = aft_ref[0:WIDE, lanes].astype(F32)
    for j in range(width // length):
        rows = other_ref.shape[0] * length // width
        pack_ref[length:, j * length : (j + 1) * length] = other_ref[j * rows : (j + 1) * rows, :]
    off = WIDE - taps // 2

    def step(i, carry):
        r0 = pl.multiple_of(i * ROWS, ROWS)
        normed, inv = normalised(convolved(win, r0 + off, seg_ref, r0 + off, kern_ref, ROWS), width)
        inv_ref[pl.ds(r0, ROWS), :] = jnp.broadcast_to(inv, (ROWS, LANES))
        for b in range(blocks):
            lanes = slice(b * LANES, (b + 1) * LANES)
            norm_ref[pl.ds(r0, ROWS), lanes] = normed[b]
            gated = normed[b] * gain_ref[:, lanes]
            pack_ref[pl.ds(r0, ROWS), lanes] = (gated * jax.nn.sigmoid(gated)).astype(BF)
        return carry

    lax.fori_loop(0, length // ROWS, step, 0)


def product_kernel(own, mine_ref, pack_ref, pack2_ref, small_ref, small2_ref, out_hbm, out_ref, sems):
    rows, length = mine_ref.shape
    width = pack_ref.shape[1]
    count = rows // own
    part = 256
    deep = rows * length // width
    got = [pack2_ref[length:, j * length : (j + 1) * length] for j in range(rows // deep)]
    got = jnp.concatenate(got, axis=0)
    copies = []

    def send(first, last):
        at = slice(first, last)
        copies.append(pltpu.make_async_copy(out_ref.at[:, at], out_hbm.at[:, at], sems.at[len(copies)]))
        copies[-1].start()

    line = width // LANES * own
    small = (small_ref[...] + small2_ref[...]).astype(BF)
    out_ref[:, line:, :] = small.reshape(count, own // 2, LANES)
    send(line, line + own // 2)
    for n in range(width // part):
        at = slice(n * part, (n + 1) * part)
        total = jnp.dot(mine_ref[...], pack_ref[0:length, at], preferred_element_type=F32)
        total = total + jnp.dot(got, pack2_ref[0:length, at], preferred_element_type=F32)
        total = total.astype(BF).reshape(count, own, part)
        for b in range(part // LANES):
            line = (n * (part // LANES) + b) * own
            out_ref[:, line : line + own, :] = total[:, :, b * LANES : (b + 1) * LANES]
        send(n * (part // LANES) * own, (n + 1) * (part // LANES) * own)
    for copy in copies:
        copy.wait()


def taps_kernel(
    own, ga_ref, norm_ref, inv_ref, gain_ref, seg_ref, win,
    gm_hbm, mine_ref, other_ref, kacc, gg_ref, gm_ref, sems,
):
    length, width = norm_ref.shape
    taps = kacc.shape[0]
    blocks = width // LANES
    group = 4
    off = WIDE - taps // 2
    gg_ref[...] = jnp.zeros(gg_ref.shape, F32)
    kacc[...] = jnp.zeros(kacc.shape, F32)

    def rows_of(value):
        rows8 = value[0:8]
        for r in range(8, ROWS, 8):
            rows8 = rows8 + value[r : r + 8]
        return rows8

    def step(i, carry):
        r0 = pl.multiple_of(i * ROWS, ROWS)
        at = pl.ds(r0, ROWS)
        sum_a = jnp.zeros((ROWS, LANES), F32)
        sum_b = jnp.zeros((ROWS, LANES), F32)
        for b in range(blocks):
            lanes = slice(b * LANES, (b + 1) * LANES)
            gain = gain_ref[:, lanes]
            normed = norm_ref[at, lanes]
            gg = gate_back(ga_ref[at, lanes], normed, gain)
            gg_ref[:, lanes] = gg_ref[:, lanes] + rows_of(gg * normed)
            gn = gg * gain
            sum_a = sum_a + gn
            sum_b = sum_b + gn * normed
            gm_ref[at, lanes] = gn
        mean_a = jnp.sum(sum_a, axis=1, keepdims=True) * (1.0 / width)
        mean_b = jnp.sum(sum_b, axis=1, keepdims=True) * (1.0 / width)
        inv = inv_ref[at, :]
        centre = seg_ref[pl.ds(r0 + WIDE, ROWS), :]
        for g in range(blocks // group):
            grads = {}
            for b in range(g * group, (g + 1) * group):
                lanes = slice(b * LANES, (b + 1) * LANES)
                grads[b] = inv * (gm_ref[at, lanes] - mean_a - norm_ref[at, lanes] * mean_b)
                gm_ref[at, lanes] = grads[b]
            for k in range(taps):
                same = seg_ref[pl.ds(r0 + off + k, ROWS), :] == centre
                for b, grad in grads.items():
                    lanes = slice(b * LANES, (b + 1) * LANES)
                    prod = jnp.where(same, win[b, pl.ds(r0 + off + k, ROWS), :], 0.0) * grad
                    kacc[k, :, lanes] = kacc[k, :, lanes] + rows_of(prod)
        pltpu.make_async_copy(gm_ref.at[at], gm_hbm.at[at], sems.at[i]).start()
        return carry

    count = length // ROWS
    lax.fori_loop(0, count, step, 0)
    core = lax.axis_index("core")
    half = own // 2
    upper = (lax.broadcasted_iota(jnp.int32, (taps + 1, LANES), 1) // half) % 2 == 1
    for b in range(blocks):
        lanes = slice(b * LANES, (b + 1) * LANES)
        rows = [jnp.sum(kacc[k, :, lanes], axis=0, keepdims=True) for k in range(taps)]
        rows.append(jnp.sum(gg_ref[:, lanes], axis=0, keepdims=True))
        rows = jnp.concatenate(rows, axis=0)
        pad = jnp.zeros((LANES - 2 * (taps + 1), LANES), F32)
        turned = jnp.concatenate([jnp.where(upper, 0.0, rows), jnp.where(upper, rows, 0.0), pad], axis=0).T
        for j in range(LANES // (2 * own)):
            at = 2 * own * j
            even = turned[at : at + half] + turned[at + half : at + own]
            odd = turned[at + own : at + own + half] + turned[at + own + half : at + 2 * own]
            deal(core, (b * (LANES // (2 * own)) + j) * half, even, odd, mine_ref, other_ref)
    for i in range(count):
        at = pl.ds(i * ROWS, ROWS)
        pltpu.make_async_copy(gm_ref.at[at], gm_hbm.at[at], sems.at[i]).wait()


def back_kernel(
    pack_ref, proj_ref, gm_ref, bef_ref, aft_ref, seg_ref, kern_ref, gain_ref, hid_hbm,
    out_ref, gh_ref, gwin, hwin, hid_ref, ga_ref, sems,
):
    taps, width = kern_ref.shape
    length = gh_ref.shape[0]
    blocks = width // LANES
    copies = (
        pltpu.make_async_copy(hid_hbm.at[0:WIDE], hid_ref.at[0], sems.at[0]),
        pltpu.make_async_copy(hid_hbm.at[length - WIDE : length], hid_ref.at[1], sems.at[1]),
    )
    for copy in copies:
        copy.start()
    matmul_into(out_ref, ((pack_ref.at[0:length], proj_ref),), transposed=True)
    matmul_into(ga_ref.at[0:NEAR], ((bef_ref.at[WIDE:], proj_ref),))
    matmul_into(ga_ref.at[NEAR:], ((aft_ref.at[WIDE:], proj_ref),))
    for copy in copies:
        copy.wait()
    for b in range(blocks):
        lanes = slice(b * LANES, (b + 1) * LANES)
        gwin[b, NEAR : NEAR + length, :] = gm_ref[:, lanes]
        hwin[b, 0:WIDE, :] = bef_ref[0:WIDE, lanes].astype(F32)
        hwin[b, WIDE : 2 * WIDE, :] = hid_ref[0, :, lanes].astype(F32)
        hwin[b, 2 * WIDE : 3 * WIDE, :] = hid_ref[1, :, lanes].astype(F32)
        hwin[b, 3 * WIDE :, :] = aft_ref[0:WIDE, lanes].astype(F32)
    reach = taps // 2
    sides = (
        (NEAR - reach, NEAR - reach, 0, 0),
        (3 * WIDE - reach, WIDE + length - reach, NEAR, NEAR + length),
    )
    for wr, sr, ar, to in sides:
        normed, inv = normalised(convolved(hwin, wr, seg_ref, sr, kern_ref, NEAR), width)
        grads = []
        for b in range(blocks):
            lanes = slice(b * LANES, (b + 1) * LANES)
            gain = gain_ref[:, lanes]
            grads.append(gate_back(ga_ref[ar : ar + NEAR, lanes], normed[b], gain) * gain)
        mean_a = mean_of(grads, width)
        mean_b = mean_of([g * n for g, n in zip(grads, normed)], width)
        for b in range(blocks):
            gwin[b, to : to + NEAR, :] = inv * (grads[b] - mean_a - normed[b] * mean_b)

    def step(i, carry):
        r0 = pl.multiple_of(i * ROWS, ROWS)
        centre = seg_ref[pl.ds(r0 + WIDE, ROWS), :]
        acc = [jnp.zeros((ROWS, LANES), F32) for _ in range(blocks)]
        for k in range(taps):
            line = NEAR + reach - k
            same = seg_ref[pl.ds(r0 + line + WIDE - NEAR, ROWS), :] == centre
            for b in range(blocks):
                w = kern_ref[k : k + 1, b * LANES : (b + 1) * LANES]
                term = gwin[b, pl.ds(r0 + line, ROWS), :] * w
                acc[b] = acc[b] + jnp.where(same, term, 0.0)
        for b in range(blocks):
            gh_ref[pl.ds(r0, ROWS), b * LANES : (b + 1) * LANES] = acc[b].astype(BF)
        return carry

    lax.fori_loop(0, length // ROWS, step, 0)


def add_kernel(landed_ref, out_ref):
    total = landed_ref[0].astype(F32)
    for j in range(1, landed_ref.shape[0]):
        total = total + landed_ref[j].astype(F32)
    out_ref[...] = total.astype(BF)


def final_kernel(factor, taps, all_ref, weight_ref, small_ref, gain_ref):
    total = all_ref[0].astype(F32)
    for j in range(1, all_ref.shape[0]):
        total = total + all_ref[j].astype(F32)
    total = total * factor
    own, width = weight_ref.shape
    for b in range(width // LANES):
        weight_ref[:, b * LANES : (b + 1) * LANES] = total[b * own : (b + 1) * own, :]
    tail = total[width // LANES * own :, :]
    tail = jnp.concatenate([tail[:, : taps + 1], tail[:, taps + 1 : 2 * (taps + 1)]], axis=0)
    small_ref[...] = tail[:, :taps]
    wide = jnp.concatenate([tail, jnp.zeros((own, LANES - taps - 1), F32)], axis=1)
    gain_ref[...] = wide.T[taps : taps + 1, :]


SEQ = ("y", "x", "core")


def shifted(value, steps):
    count = lax.axis_size("y") * lax.axis_size("x") * lax.axis_size("core")
    first, last = max(0, -steps), min(count, count - steps)
    return lax.ppermute(value, SEQ, [(i, i + steps) for i in range(first, last)])


def inner(hidden, segment_ids, kernel, norm_gain, projection, cotangent):
    frames = hidden[0]
    length, width = frames.shape
    taps = kernel.shape[0]
    cot = cotangent[0]
    ny, nx = lax.axis_size("y"), lax.axis_size("x")
    own = width // (ny * nx * 2)
    swap = [(0, 1), (1, 0)]
    big = 2 * length * width * width
    vec = length * width * taps
    shape = jax.ShapeDtypeStruct
    rows_win = length + 2 * WIDE
    blocks = width // LANES
    window = (blocks, rows_win, LANES)
    lines = (blocks * own) + own // 2

    message = shape((WIDE + NEAR, width), BF)
    up, down = call(
        ends_kernel, (message, message), [pltpu.SemaphoreType.DMA((4,))], moved=512 * width, hbm=(0, 1)
    )(frames, cot)
    before = shifted(up, 1)
    after = shifted(down, -1)
    half = shape((width // 2, length), BF)
    ids = segment_ids.reshape(-1, LANES)
    mine, other, seg, mid, grad_act, kern, gain = call(
        partial(first_kernel, own),
        (
            half,
            half,
            shape((rows_win, LANES), F32),
            shape((blocks, length, LANES), F32),
            shape((length, width), F32),
            shape((taps, width), F32),
            shape((1, width), F32),
        ),
        [
            pltpu.VMEM(ids.shape, ids.dtype),
            pltpu.VMEM((length, width), BF),
            pltpu.VMEM((length, width), BF),
            pltpu.VMEM((width, width), BF),
            pltpu.SemaphoreType.DMA((6,)),
        ],
        flops=big,
        moved=12 * length * width,
        hbm=range(6),
    )(ids, cot, frames, projection, kernel, norm_gain[None, :])
    pack, normed, inv, win = call(
        forward_kernel,
        (
            shape((length + length // 2, width), BF),
            shape((length, width), F32),
            shape((length, LANES), F32),
            shape(window, F32),
        ),
        flops=3 * vec,
        moved=8 * length * width,
        trans=2 * length * width,
    )(mid, before, after, seg, kern, gain, other)
    pack2 = lax.ppermute(pack, "core", swap)
    dealt = shape((width // 4, LANES), F32)
    grad_mixed, small, small_other = call(
        partial(taps_kernel, own),
        (pltpu.HBM((length, width), F32), dealt, dealt),
        [
            pltpu.VMEM((taps, 8, width), F32),
            pltpu.VMEM((8, width), F32),
            pltpu.VMEM((length, width), F32),
            pltpu.SemaphoreType.DMA((length // ROWS,)),
        ],
        far=1,
        flops=3 * vec,
        moved=16 * length * width,
        trans=2 * length * width,
    )(grad_act, normed, inv, gain, seg, win)
    small2 = lax.ppermute(small_other, "core", swap)
    weight = call(
        partial(product_kernel, own),
        pltpu.HBM((ny * nx, lines, LANES), BF),
        [pltpu.VMEM((ny * nx, lines, LANES), BF), pltpu.SemaphoreType.DMA((width // 256 + 1,))],
        far=1,
        flops=big,
        moved=2 * (width * width + 3 * length * width),
    )(mine, pack, pack2, small, small2)
    landed = lax.all_to_all(weight, ("y", "x"), split_axis=0, concat_axis=0, tiled=True)
    conv_out, grad_hidden = call(
        back_kernel,
        (shape((length, width), BF), shape((length, width), BF)),
        [
            pltpu.VMEM((blocks, length + 2 * NEAR, LANES), F32),
            pltpu.VMEM((blocks, 4 * WIDE, LANES), F32),
            pltpu.VMEM((2, WIDE, width), BF),
            pltpu.VMEM((2 * NEAR, width), F32),
            pltpu.SemaphoreType.DMA((2,)),
        ],
        flops=3 * vec + big,
        moved=12 * length * width,
        hbm=(8,),
    )(pack, projection, grad_mixed, before, after, seg, kern, gain, frames)
    share = call(add_kernel, shape((lines, LANES), BF), moved=80 * own * width)(landed)
    everyone = lax.all_gather(share, "dp")
    factor = 1.0 / math.sqrt(length * ny * nx * 2 * lax.axis_size("dp"))
    grad_weight, grad_kernel, grad_gain = call(
        partial(final_kernel, factor, taps),
        (shape((own, width), F32), shape((own, taps), F32), shape((1, own), F32)),
        moved=64 * own * width,
    )(everyone)
    return conv_out[None], grad_hidden[None], grad_weight, grad_kernel, grad_gain[0]


def solution(mesh):
    dp, seq = mesh.devices.shape
    fine = Mesh(mesh.devices.reshape(dp, 8, seq // 16, 2), ("dp",) + SEQ)
    rows = P("dp", SEQ, None)
    in_specs = (rows, P("dp", None), P(), P(), P(), rows)
    out_specs = (rows, rows, P(SEQ, None), P(SEQ, None), P(SEQ))
    return jax.shard_map(inner, mesh=fine, in_specs=in_specs, out_specs=out_specs, check_vma=False)
```

```python
import math
from functools import partial

import jax
import jax.numpy as jnp
from jax import lax
from jax.experimental import pallas as pl
from jax.experimental.pallas import tpu as pltpu
from jax.sharding import Mesh
from jax.sharding import PartitionSpec as P


EPS = 1e-05
LANES = 128
NEAR = 16
WIDE = 32
ROWS = 32
GROUP = 4
BF = jnp.bfloat16
F32 = jnp.float32


def call(kernel, outs, scratch=(), flops=0, moved=0, trans=0, hbm=(), far=0, limit=9):
    def run(*args):
        specs = [
            pl.BlockSpec(memory_space=pltpu.HBM if i in hbm else pltpu.VMEM)
            for i in range(len(args))
        ]
        args = [
            pltpu.with_memory_space_constraint(arg, pltpu.HBM) if i in hbm else arg
            for i, arg in enumerate(args)
        ]
        return pl.pallas_call(
            kernel,
            out_shape=outs,
            in_specs=specs,
            out_specs=jax.tree.unflatten(
                jax.tree.structure(outs),
                [
                    pl.BlockSpec(memory_space=pltpu.HBM if i < far else pltpu.VMEM)
                    for i in range(len(jax.tree.leaves(outs)))
                ],
            ),
            scratch_shapes=list(scratch),
            compiler_params=pltpu.CompilerParams(vmem_limit_bytes=limit * 1024 * 1024),
            cost_estimate=pl.CostEstimate(flops=flops, bytes_accessed=moved, transcendentals=trans),
        )(*args)

    return run


def deal(core, at, even, odd, mine_ref, other_ref):
    mine_ref[at : at + even.shape[0], :] = jnp.where(core == 0, even, odd)
    other_ref[at : at + even.shape[0], :] = jnp.where(core == 0, odd, even)


def place_of(axes):
    index = lax.axis_index(axes[0])
    for axis in axes[1:]:
        index = index * lax.axis_size(axis) + lax.axis_index(axis)
    return index


def matmul_into(out_ref, pairs, transposed=False):
    part = 256
    dims = (((1,), (1,)), ((), ())) if transposed else (((1,), (0,)), ((), ()))
    for n in range(out_ref.shape[1] // part):
        at = slice(n * part, (n + 1) * part)
        total = None
        for left, right in pairs:
            term = lax.dot_general(
                left[...], right[at, :] if transposed else right[:, at], dims, preferred_element_type=F32
            )
            total = term if total is None else total + term
        out_ref[:, at] = total.astype(out_ref.dtype)


def ends_kernel(hid_hbm, cot_hbm, up_ref, down_ref, sems):
    length = hid_hbm.shape[0]
    pairs = (
        (hid_hbm.at[length - WIDE : length], up_ref.at[0:WIDE]),
        (cot_hbm.at[length - NEAR : length], up_ref.at[WIDE : WIDE + NEAR]),
        (hid_hbm.at[0:WIDE], down_ref.at[0:WIDE]),
        (cot_hbm.at[0:NEAR], down_ref.at[WIDE : WIDE + NEAR]),
    )
    copies = [pltpu.make_async_copy(src, dst, sems.at[i]) for i, (src, dst) in enumerate(pairs)]
    for copy in copies:
        copy.start()
    for copy in copies:
        copy.wait()


def first_kernel(
    own, ids_hbm, cot_hbm, hid_hbm, proj_hbm, kern_hbm, gain_hbm,
    mine_ref, other_ref, seg_ref, mid_ref, ga_ref, kern_ref, gain_ref,
    ids_ref, cot_ref, hid_ref, proj_ref, sems,
):
    pairs = (
        (cot_hbm, cot_ref), (ids_hbm, ids_ref), (hid_hbm, hid_ref),
        (kern_hbm, kern_ref), (gain_hbm, gain_ref), (proj_hbm, proj_ref),
    )
    copies = [pltpu.make_async_copy(src, dst, sems.at[i]) for i, (src, dst) in enumerate(pairs)]
    for copy in copies:
        copy.start()
    copies[0].wait()
    core = lax.axis_index("core")
    length, width = cot_ref.shape
    for b in range(width // LANES):
        turned = cot_ref[:, b * LANES : (b + 1) * LANES].T
        for j in range(LANES // (2 * own)):
            at = 2 * own * j
            even, odd = turned[at : at + own], turned[at + own : at + 2 * own]
            deal(core, (b * (LANES // (2 * own)) + j) * own, even, odd, mine_ref, other_ref)
    copies[1].wait()
    index = place_of(SEQ)
    lines = length // LANES
    last = ids_ref.shape[0] - 1

    def column(line, outside):
        row = ids_ref[pl.ds(jnp.clip(line, 0, last), 1), :].astype(F32)
        square = jnp.broadcast_to(row, (LANES, LANES)).T
        return jnp.where(outside, -1.0, square)

    head = column(lines * index - 1, index == 0)
    seg_ref[0:WIDE, :] = head[LANES - WIDE :]
    for j in range(lines):
        seg_ref[WIDE + j * LANES : WIDE + (j + 1) * LANES, :] = column(lines * index + j, False)
    tail = column(lines * index + lines, lines * index + lines > last)
    seg_ref[WIDE + length : 2 * WIDE + length, :] = tail[:WIDE]
    copies[2].wait()
    for b in range(width // LANES):
        mid_ref[b] = hid_ref[:, b * LANES : (b + 1) * LANES].astype(F32)
    for copy in copies[3:]:
        copy.wait()
    matmul_into(ga_ref, ((cot_ref, proj_ref),))


def convolved(win, wr, seg_ref, sr, kern_ref, rows, flipped=False):
    taps, width = kern_ref.shape
    blocks = width // LANES
    centre = seg_ref[pl.ds(sr + taps // 2, rows), :]
    acc = [jnp.zeros((rows, LANES), F32) for _ in range(blocks)]
    for g in range(0, blocks, GROUP):
        for shift in range(8):
            own = range(shift, taps, 8)
            deep = rows + 8 * (len(own) - 1)
            segs = seg_ref[pl.ds(sr + shift, deep), :]
            wins = {b: win[b, pl.ds(wr + shift, deep), :] for b in range(g, g + GROUP)}
            for q, k in enumerate(own):
                same = segs[8 * q : 8 * q + rows] == centre
                tap = taps - 1 - k if flipped else k
                for b, lot in wins.items():
                    term = lot[8 * q : 8 * q + rows] * kern_ref[tap : tap + 1, b * LANES : (b + 1) * LANES]
                    acc[b] = acc[b] + jnp.where(same, term, 0.0)
    return acc


def mean_of(parts, width):
    total = parts[0]
    for part in parts[1:]:
        total = total + part
    return jnp.sum(total, axis=1, keepdims=True) * (1.0 / width)


def normalised(acc, width):
    mean = mean_of(acc, width)
    acc = [a - mean for a in acc]
    inv = lax.rsqrt(mean_of([a * a for a in acc], width) + EPS)
    return [a * inv for a in acc], inv


def gate_back(grad, normed, gain):
    gated = normed * gain
    sigma = jax.nn.sigmoid(gated)
    return grad * sigma * (1.0 + gated * (1.0 - sigma))


def forward_kernel(
    mid_ref, bef_ref, aft_ref, seg_ref, kern_ref, gain_ref, other_ref, pack_ref, norm_ref, inv_ref, win
):
    taps, width = kern_ref.shape
    length = norm_ref.shape[0]
    blocks = width // LANES
    for b in range(blocks):
        lanes = slice(b * LANES, (b + 1) * LANES)
        win[b, 0:WIDE, :] = bef_ref[0:WIDE, lanes].astype(F32)
        win[b, WIDE : WIDE + length, :] = mid_ref[b]
        win[b, WIDE + length :, :] = aft_ref[0:WIDE, lanes].astype(F32)
    for j in range(width // length):
        rows = other_ref.shape[0] * length // width
        pack_ref[length:, j * length : (j + 1) * length] = other_ref[j * rows : (j + 1) * rows, :]
    off = WIDE - taps // 2

    def step(i, carry):
        r0 = pl.multiple_of(i * ROWS, ROWS)
        normed, inv = normalised(convolved(win, r0 + off, seg_ref, r0 + off, kern_ref, ROWS), width)
        inv_ref[pl.ds(r0, ROWS), :] = jnp.broadcast_to(inv, (ROWS, LANES))
        for b in range(blocks):
            lanes = slice(b * LANES, (b + 1) * LANES)
            norm_ref[pl.ds(r0, ROWS), lanes] = normed[b]
            gated = normed[b] * gain_ref[:, lanes]
            pack_ref[pl.ds(r0, ROWS), lanes] = (gated * jax.nn.sigmoid(gated)).astype(BF)
        return carry

    lax.fori_loop(0, length // ROWS, step, 0)


def product_kernel(own, mine_ref, pack_ref, pack2_ref, small_ref, small2_ref, out_hbm, out_ref, sems):
    rows, length = mine_ref.shape
    width = pack_ref.shape[1]
    count = rows // own
    part = 256
    deep = rows * length // width
    got = [pack2_ref[length:, j * length : (j + 1) * length] for j in range(rows // deep)]
    got = jnp.concatenate(got, axis=0)
    copies = []

    def send(first, last):
        at = slice(first, last)
        copies.append(pltpu.make_async_copy(out_ref.at[:, at], out_hbm.at[:, at], sems.at[len(copies)]))
        copies[-1].start()

    line = width // LANES * own
    small = (small_ref[...] + small2_ref[...]).astype(BF)
    out_ref[:, line:, :] = small.reshape(count, own // 2, LANES)
    send(line, line + own // 2)
    for n in range(width // part):
        at = slice(n * part, (n + 1) * part)
        total = jnp.dot(mine_ref[...], pack_ref[0:length, at], preferred_element_type=F32)
        total = total + jnp.dot(got, pack2_ref[0:length, at], preferred_element_type=F32)
        total = total.astype(BF).reshape(count, own, part)
        for b in range(part // LANES):
            line = (n * (part // LANES) + b) * own
            out_ref[:, line : line + own, :] = total[:, :, b * LANES : (b + 1) * LANES]
        send(n * (part // LANES) * own, (n + 1) * (part // LANES) * own)
    for copy in copies:
        copy.wait()


def taps_kernel(
    own, ga_ref, norm_ref, inv_ref, gain_ref, seg_ref, win,
    gm_hbm, mine_ref, other_ref, kacc, gg_ref, gm_ref, sems,
):
    length, width = norm_ref.shape
    taps = kacc.shape[0]
    blocks = width // LANES
    group = 4
    off = WIDE - taps // 2
    gg_ref[...] = jnp.zeros(gg_ref.shape, F32)
    kacc[...] = jnp.zeros(kacc.shape, F32)

    def rows_of(value):
        rows8 = value[0:8]
        for r in range(8, ROWS, 8):
            rows8 = rows8 + value[r : r + 8]
        return rows8

    def step(i, carry):
        r0 = pl.multiple_of(i * ROWS, ROWS)
        at = pl.ds(r0, ROWS)
        sum_a = jnp.zeros((ROWS, LANES), F32)
        sum_b = jnp.zeros((ROWS, LANES), F32)
        for b in range(blocks):
            lanes = slice(b * LANES, (b + 1) * LANES)
            gain = gain_ref[:, lanes]
            normed = norm_ref[at, lanes]
            gg = gate_back(ga_ref[at, lanes], normed, gain)
            gg_ref[:, lanes] = gg_ref[:, lanes] + rows_of(gg * normed)
            gn = gg * gain
            sum_a = sum_a + gn
            sum_b = sum_b + gn * normed
            gm_ref[at, lanes] = gn
        mean_a = jnp.sum(sum_a, axis=1, keepdims=True) * (1.0 / width)
        mean_b = jnp.sum(sum_b, axis=1, keepdims=True) * (1.0 / width)
        inv = inv_ref[at, :]
        centre = seg_ref[pl.ds(r0 + WIDE, ROWS), :]
        for g in range(blocks // group):
            grads = {}
            for b in range(g * group, (g + 1) * group):
                lanes = slice(b * LANES, (b + 1) * LANES)
                grads[b] = inv * (gm_ref[at, lanes] - mean_a - norm_ref[at, lanes] * mean_b)
                gm_ref[at, lanes] = grads[b]
            for shift in range(8):
                ks = range(shift, taps, 8)
                deep = ROWS + 8 * (len(ks) - 1)
                segs = seg_ref[pl.ds(r0 + off + shift, deep), :]
                wins = {b: win[b, pl.ds(r0 + off + shift, deep), :] for b in grads}
                for q, k in enumerate(ks):
                    same = segs[8 * q : 8 * q + ROWS] == centre
                    for b, grad in grads.items():
                        lanes = slice(b * LANES, (b + 1) * LANES)
                        prod = jnp.where(same, wins[b][8 * q : 8 * q + ROWS], 0.0) * grad
                        kacc[k, :, lanes] = kacc[k, :, lanes] + rows_of(prod)
        pltpu.make_async_copy(gm_ref.at[at], gm_hbm.at[at], sems.at[i]).start()
        return carry

    count = length // ROWS
    lax.fori_loop(0, count, step, 0)
    core = lax.axis_index("core")
    half = own // 2
    upper = (lax.broadcasted_iota(jnp.int32, (taps + 1, LANES), 1) // half) % 2 == 1
    for b in range(blocks):
        lanes = slice(b * LANES, (b + 1) * LANES)
        rows = [jnp.sum(kacc[k, :, lanes], axis=0, keepdims=True) for k in range(taps)]
        rows.append(jnp.sum(gg_ref[:, lanes], axis=0, keepdims=True))
        rows = jnp.concatenate(rows, axis=0)
        pad = jnp.zeros((LANES - 2 * (taps + 1), LANES), F32)
        turned = jnp.concatenate([jnp.where(upper, 0.0, rows), jnp.where(upper, rows, 0.0), pad], axis=0).T
        for j in range(LANES // (2 * own)):
            at = 2 * own * j
            even = turned[at : at + half] + turned[at + half : at + own]
            odd = turned[at + own : at + own + half] + turned[at + own + half : at + 2 * own]
            deal(core, (b * (LANES // (2 * own)) + j) * half, even, odd, mine_ref, other_ref)
    for i in range(count):
        at = pl.ds(i * ROWS, ROWS)
        pltpu.make_async_copy(gm_ref.at[at], gm_hbm.at[at], sems.at[i]).wait()


def back_kernel(
    pack_ref, proj_ref, gm_ref, bef_ref, aft_ref, seg_ref, kern_ref, gain_ref, hid_hbm,
    out_ref, gh_ref, gwin, hwin, hid_ref, ga_ref, sems,
):
    taps, width = kern_ref.shape
    length = gh_ref.shape[0]
    blocks = width // LANES
    copies = (
        pltpu.make_async_copy(hid_hbm.at[0:WIDE], hid_ref.at[0], sems.at[0]),
        pltpu.make_async_copy(hid_hbm.at[length - WIDE : length], hid_ref.at[1], sems.at[1]),
    )
    for copy in copies:
        copy.start()
    matmul_into(out_ref, ((pack_ref.at[0:length], proj_ref),), transposed=True)
    matmul_into(ga_ref.at[0:NEAR], ((bef_ref.at[WIDE:], proj_ref),))
    matmul_into(ga_ref.at[NEAR:], ((aft_ref.at[WIDE:], proj_ref),))
    for copy in copies:
        copy.wait()
    for b in range(blocks):
        lanes = slice(b * LANES, (b + 1) * LANES)
        gwin[b, NEAR : NEAR + length, :] = gm_ref[:, lanes]
        hwin[b, 0:WIDE, :] = bef_ref[0:WIDE, lanes].astype(F32)
        hwin[b, WIDE : 2 * WIDE, :] = hid_ref[0, :, lanes].astype(F32)
        hwin[b, 2 * WIDE : 3 * WIDE, :] = hid_ref[1, :, lanes].astype(F32)
        hwin[b, 3 * WIDE :, :] = aft_ref[0:WIDE, lanes].astype(F32)
    reach = taps // 2
    sides = (
        (NEAR - reach, NEAR - reach, 0, 0),
        (3 * WIDE - reach, WIDE + length - reach, NEAR, NEAR + length),
    )
    for wr, sr, ar, to in sides:
        normed, inv = normalised(convolved(hwin, wr, seg_ref, sr, kern_ref, NEAR), width)
        grads = []
        for b in range(blocks):
            lanes = slice(b * LANES, (b + 1) * LANES)
            gain = gain_ref[:, lanes]
            grads.append(gate_back(ga_ref[ar : ar + NEAR, lanes], normed[b], gain) * gain)
        mean_a = mean_of(grads, width)
        mean_b = mean_of([g * n for g, n in zip(grads, normed)], width)
        for b in range(blocks):
            gwin[b, to : to + NEAR, :] = inv * (grads[b] - mean_a - normed[b] * mean_b)

    def step(i, carry):
        r0 = pl.multiple_of(i * ROWS, ROWS)
        acc = convolved(gwin, r0 + NEAR - reach, seg_ref, r0 + WIDE - reach, kern_ref, ROWS, True)
        for b in range(blocks):
            gh_ref[pl.ds(r0, ROWS), b * LANES : (b + 1) * LANES] = acc[b].astype(BF)
        return carry

    lax.fori_loop(0, length // ROWS, step, 0)


def add_kernel(landed_ref, out_ref):
    total = landed_ref[0].astype(F32)
    for j in range(1, landed_ref.shape[0]):
        total = total + landed_ref[j].astype(F32)
    total = total.astype(BF)
    for j in range(out_ref.shape[0]):
        out_ref[j] = total


def final_kernel(factor, taps, all_ref, weight_ref, small_ref, gain_ref):
    total = all_ref[0].astype(F32)
    for j in range(1, all_ref.shape[0]):
        total = total + all_ref[j].astype(F32)
    total = total * factor
    own, width = weight_ref.shape
    for b in range(width // LANES):
        weight_ref[:, b * LANES : (b + 1) * LANES] = total[b * own : (b + 1) * own, :]
    tail = total[width // LANES * own :, :]
    tail = jnp.concatenate([tail[:, : taps + 1], tail[:, taps + 1 : 2 * (taps + 1)]], axis=0)
    small_ref[...] = tail[:, :taps]
    wide = jnp.concatenate([tail, jnp.zeros((own, LANES - taps - 1), F32)], axis=1)
    gain_ref[...] = wide.T[taps : taps + 1, :]


SEQ = ("y", "x", "core")
Z = ("zfar", "znear")


def shifted(value, steps):
    count = lax.axis_size("y") * lax.axis_size("x") * lax.axis_size("core")
    first, last = max(0, -steps), min(count, count - steps)
    return lax.ppermute(value, SEQ, [(i, i + steps) for i in range(first, last)])


def inner(hidden, segment_ids, kernel, norm_gain, projection, cotangent):
    frames = hidden[0]
    length, width = frames.shape
    taps = kernel.shape[0]
    cot = cotangent[0]
    ny, nx = lax.axis_size("y"), lax.axis_size("x")
    own = width // (ny * nx * 2)
    swap = [(0, 1), (1, 0)]
    big = 2 * length * width * width
    vec = length * width * taps
    shape = jax.ShapeDtypeStruct
    rows_win = length + 2 * WIDE
    blocks = width // LANES
    window = (blocks, rows_win, LANES)
    lines = (blocks * own) + own // 2

    message = shape((WIDE + NEAR, width), BF)
    up, down = call(
        ends_kernel, (message, message), [pltpu.SemaphoreType.DMA((4,))], moved=512 * width, hbm=(0, 1)
    )(frames, cot)
    before = shifted(up, 1)
    after = shifted(down, -1)
    half = shape((width // 2, length), BF)
    ids = segment_ids.reshape(-1, LANES)
    mine, other, seg, mid, grad_act, kern, gain = call(
        partial(first_kernel, own),
        (
            half,
            half,
            shape((rows_win, LANES), F32),
            shape((blocks, length, LANES), F32),
            shape((length, width), F32),
            shape((taps, width), F32),
            shape((1, width), F32),
        ),
        [
            pltpu.VMEM(ids.shape, ids.dtype),
            pltpu.VMEM((length, width), BF),
            pltpu.VMEM((length, width), BF),
            pltpu.VMEM((width, width), BF),
            pltpu.SemaphoreType.DMA((6,)),
        ],
        flops=big,
        moved=12 * length * width,
        hbm=range(6),
    )(ids, cot, frames, projection, kernel, norm_gain[None, :])
    pack, normed, inv, win = call(
        forward_kernel,
        (
            shape((length + length // 2, width), BF),
            shape((length, width), F32),
            shape((length, LANES), F32),
            shape(window, F32),
        ),
        flops=3 * vec,
        moved=8 * length * width,
        trans=2 * length * width,
    )(mid, before, after, seg, kern, gain, other)
    pack2 = lax.ppermute(pack, "core", swap)
    dealt = shape((width // 4, LANES), F32)
    grad_mixed, small, small_other = call(
        partial(taps_kernel, own),
        (pltpu.HBM((length, width), F32), dealt, dealt),
        [
            pltpu.VMEM((taps, 8, width), F32),
            pltpu.VMEM((8, width), F32),
            pltpu.VMEM((length, width), F32),
            pltpu.SemaphoreType.DMA((length // ROWS,)),
        ],
        far=1,
        flops=3 * vec,
        moved=16 * length * width,
        trans=2 * length * width,
    )(grad_act, normed, inv, gain, seg, win)
    small2 = lax.ppermute(small_other, "core", swap)
    weight = call(
        partial(product_kernel, own),
        pltpu.HBM((ny * nx, lines, LANES), BF),
        [pltpu.VMEM((ny * nx, lines, LANES), BF), pltpu.SemaphoreType.DMA((width // 256 + 1,))],
        far=1,
        flops=big,
        moved=2 * (width * width + 3 * length * width),
    )(mine, pack, pack2, small, small2)
    landed = lax.all_to_all(weight, ("y", "x"), split_axis=0, concat_axis=0, tiled=True)
    conv_out, grad_hidden = call(
        back_kernel,
        (shape((length, width), BF), shape((length, width), BF)),
        [
            pltpu.VMEM((blocks, length + 2 * NEAR, LANES), F32),
            pltpu.VMEM((blocks, 4 * WIDE, LANES), F32),
            pltpu.VMEM((2, WIDE, width), BF),
            pltpu.VMEM((2 * NEAR, width), F32),
            pltpu.SemaphoreType.DMA((2,)),
        ],
        flops=3 * vec + big,
        moved=12 * length * width,
        hbm=(8,),
    )(pack, projection, grad_mixed, before, after, seg, kern, gain, frames)
    near, far = lax.axis_size("znear"), lax.axis_size("zfar")
    copies = call(add_kernel, shape((near, lines, LANES), BF), moved=80 * own * width)(landed)
    copies = lax.all_to_all(copies, "znear", split_axis=0, concat_axis=0, tiled=True)
    share = call(add_kernel, shape((far, lines, LANES), BF), moved=20 * own * width)(copies)
    everyone = lax.all_to_all(share, "zfar", split_axis=0, concat_axis=0, tiled=True)
    factor = 1.0 / math.sqrt(length * ny * nx * 2 * near * far)
    grad_weight, grad_kernel, grad_gain = call(
        partial(final_kernel, factor, taps),
        (shape((own, width), F32), shape((own, taps), F32), shape((1, own), F32)),
        moved=64 * own * width,
    )(everyone)
    return conv_out[None], grad_hidden[None], grad_weight, grad_kernel, grad_gain[0]


def solution(mesh):
    dp, seq = mesh.devices.shape
    fine = Mesh(mesh.devices.reshape(dp // 4, 4, 8, seq // 16, 2), Z + SEQ)
    rows = P(Z, SEQ, None)
    in_specs = (rows, P(Z, None), P(), P(), P(), rows)
    out_specs = (rows, rows, P(SEQ, None), P(SEQ, None), P(SEQ))
    return jax.shard_map(inner, mesh=fine, in_specs=in_specs, out_specs=out_specs, check_vma=False)
```

```python
import math
from functools import partial

import jax
import jax.numpy as jnp
from jax import lax
from jax.experimental import pallas as pl
from jax.experimental.pallas import tpu as pltpu
from jax.sharding import Mesh
from jax.sharding import PartitionSpec as P


EPS = 1e-05
LANES = 128
NEAR = 16
WIDE = 32
ROWS = 32
GROUP = 4
BF = jnp.bfloat16
F32 = jnp.float32


def call(kernel, outs, scratch=(), flops=0, moved=0, trans=0, hbm=(), far=0, limit=9):
    def run(*args):
        specs = [
            pl.BlockSpec(memory_space=pltpu.HBM if i in hbm else pltpu.VMEM)
            for i in range(len(args))
        ]
        args = [
            pltpu.with_memory_space_constraint(arg, pltpu.HBM) if i in hbm else arg
            for i, arg in enumerate(args)
        ]
        return pl.pallas_call(
            kernel,
            out_shape=outs,
            in_specs=specs,
            out_specs=jax.tree.unflatten(
                jax.tree.structure(outs),
                [
                    pl.BlockSpec(memory_space=pltpu.HBM if i < far else pltpu.VMEM)
                    for i in range(len(jax.tree.leaves(outs)))
                ],
            ),
            scratch_shapes=list(scratch),
            compiler_params=pltpu.CompilerParams(vmem_limit_bytes=limit * 1024 * 1024),
            cost_estimate=pl.CostEstimate(flops=flops, bytes_accessed=moved, transcendentals=trans),
        )(*args)

    return run


def deal(core, at, even, odd, mine_ref, other_ref):
    mine_ref[at : at + even.shape[0], :] = jnp.where(core == 0, even, odd)
    other_ref[at : at + even.shape[0], :] = jnp.where(core == 0, odd, even)


def place_of(axes):
    index = lax.axis_index(axes[0])
    for axis in axes[1:]:
        index = index * lax.axis_size(axis) + lax.axis_index(axis)
    return index


def matmul_into(out_ref, pairs, transposed=False):
    part = 256
    dims = (((1,), (1,)), ((), ())) if transposed else (((1,), (0,)), ((), ()))
    for n in range(out_ref.shape[1] // part):
        at = slice(n * part, (n + 1) * part)
        total = None
        for left, right in pairs:
            term = lax.dot_general(
                left[...], right[at, :] if transposed else right[:, at], dims, preferred_element_type=F32
            )
            total = term if total is None else total + term
        out_ref[:, at] = total.astype(out_ref.dtype)


def ends_kernel(hid_hbm, cot_hbm, mate_ref, outer_ref, sems):
    length = hid_hbm.shape[0]
    core = lax.axis_index("core")
    copies = []
    for end, dst in ((core == 0, mate_ref), (core == 1, outer_ref)):
        for src, rows, to in ((hid_hbm, WIDE, 0), (cot_hbm, NEAR, WIDE)):
            at = pl.multiple_of(jnp.where(end, length - rows, 0), NEAR)
            copies.append(
                pltpu.make_async_copy(src.at[pl.ds(at, rows)], dst.at[to : to + rows], sems.at[len(copies)])
            )
    for copy in copies:
        copy.start()
    for copy in copies:
        copy.wait()


def sorted_ends(mate, outer):
    core = lax.axis_index("core")
    return jnp.where(core == 0, outer, mate), jnp.where(core == 0, mate, outer)


def first_kernel(
    own, ids_hbm, cot_hbm, hid_hbm, proj_hbm, kern_hbm, gain_hbm,
    mine_ref, other_ref, seg_ref, mid_ref, ga_ref, kern_ref, gain_ref,
    ids_ref, cot_ref, hid_ref, proj_ref, sems,
):
    pairs = (
        (cot_hbm, cot_ref), (ids_hbm, ids_ref), (hid_hbm, hid_ref),
        (kern_hbm, kern_ref), (gain_hbm, gain_ref), (proj_hbm, proj_ref),
    )
    copies = [pltpu.make_async_copy(src, dst, sems.at[i]) for i, (src, dst) in enumerate(pairs)]
    for copy in copies:
        copy.start()
    copies[0].wait()
    core = lax.axis_index("core")
    length, width = cot_ref.shape
    for b in range(width // LANES):
        turned = cot_ref[:, b * LANES : (b + 1) * LANES].T
        for j in range(LANES // (2 * own)):
            at = 2 * own * j
            even, odd = turned[at : at + own], turned[at + own : at + 2 * own]
            deal(core, (b * (LANES // (2 * own)) + j) * own, even, odd, mine_ref, other_ref)
    copies[1].wait()
    index = place_of(SEQ)
    lines = length // LANES
    last = ids_ref.shape[0] - 1

    def column(line, outside):
        row = ids_ref[pl.ds(jnp.clip(line, 0, last), 1), :].astype(F32)
        square = jnp.broadcast_to(row, (LANES, LANES)).T
        return jnp.where(outside, -1.0, square)

    head = column(lines * index - 1, index == 0)
    seg_ref[0:WIDE, :] = head[LANES - WIDE :]
    for j in range(lines):
        seg_ref[WIDE + j * LANES : WIDE + (j + 1) * LANES, :] = column(lines * index + j, False)
    tail = column(lines * index + lines, lines * index + lines > last)
    seg_ref[WIDE + length : 2 * WIDE + length, :] = tail[:WIDE]
    copies[2].wait()
    for b in range(width // LANES):
        mid_ref[b] = hid_ref[:, b * LANES : (b + 1) * LANES].astype(F32)
    for copy in copies[3:]:
        copy.wait()
    matmul_into(ga_ref, ((cot_ref, proj_ref),))


def convolved(win, wr, seg_ref, sr, kern_ref, rows, flipped=False):
    taps, width = kern_ref.shape
    blocks = width // LANES
    centre = seg_ref[pl.ds(sr + taps // 2, rows), :]
    acc = [jnp.zeros((rows, LANES), F32) for _ in range(blocks)]
    for g in range(0, blocks, GROUP):
        for shift in range(8):
            own = range(shift, taps, 8)
            deep = rows + 8 * (len(own) - 1)
            segs = seg_ref[pl.ds(sr + shift, deep), :]
            wins = {b: win[b, pl.ds(wr + shift, deep), :] for b in range(g, g + GROUP)}
            for q, k in enumerate(own):
                same = segs[8 * q : 8 * q + rows] == centre
                tap = taps - 1 - k if flipped else k
                for b, lot in wins.items():
                    term = lot[8 * q : 8 * q + rows] * kern_ref[tap : tap + 1, b * LANES : (b + 1) * LANES]
                    acc[b] = acc[b] + jnp.where(same, term, 0.0)
    return acc


def mean_of(parts, width):
    total = parts[0]
    for part in parts[1:]:
        total = total + part
    return jnp.sum(total, axis=1, keepdims=True) * (1.0 / width)


def normalised(acc, width):
    mean = mean_of(acc, width)
    acc = [a - mean for a in acc]
    inv = lax.rsqrt(mean_of([a * a for a in acc], width) + EPS)
    return [a * inv for a in acc], inv


def gate_back(grad, normed, gain):
    gated = normed * gain
    sigma = jax.nn.sigmoid(gated)
    return grad * sigma * (1.0 + gated * (1.0 - sigma))


def forward_kernel(
    mid_ref, mate_ref, outer_ref, seg_ref, kern_ref, gain_ref, other_ref, pack_ref, norm_ref, inv_ref, win
):
    taps, width = kern_ref.shape
    length = norm_ref.shape[0]
    blocks = width // LANES
    for b in range(blocks):
        lanes = slice(b * LANES, (b + 1) * LANES)
        before, after = sorted_ends(mate_ref[0:WIDE, lanes].astype(F32), outer_ref[0:WIDE, lanes].astype(F32))
        win[b, 0:WIDE, :] = before
        win[b, WIDE : WIDE + length, :] = mid_ref[b]
        win[b, WIDE + length :, :] = after
    for j in range(width // length):
        rows = other_ref.shape[0] * length // width
        pack_ref[length:, j * length : (j + 1) * length] = other_ref[j * rows : (j + 1) * rows, :]
    off = WIDE - taps // 2

    def step(i, carry):
        r0 = pl.multiple_of(i * ROWS, ROWS)
        normed, inv = normalised(convolved(win, r0 + off, seg_ref, r0 + off, kern_ref, ROWS), width)
        inv_ref[pl.ds(r0, ROWS), :] = jnp.broadcast_to(inv, (ROWS, LANES))
        for b in range(blocks):
            lanes = slice(b * LANES, (b + 1) * LANES)
            norm_ref[pl.ds(r0, ROWS), lanes] = normed[b]
            gated = normed[b] * gain_ref[:, lanes]
            pack_ref[pl.ds(r0, ROWS), lanes] = (gated * jax.nn.sigmoid(gated)).astype(BF)
        return carry

    lax.fori_loop(0, length // ROWS, step, 0)


def product_kernel(own, mine_ref, pack_ref, pack2_ref, small_ref, small2_ref, out_hbm, out_ref, sems):
    rows, length = mine_ref.shape
    width = pack_ref.shape[1]
    count = rows // own
    part = 256
    deep = rows * length // width
    got = [pack2_ref[length:, j * length : (j + 1) * length] for j in range(rows // deep)]
    got = jnp.concatenate(got, axis=0)
    copies = []

    def send(first, last):
        at = slice(first, last)
        copies.append(pltpu.make_async_copy(out_ref.at[:, at], out_hbm.at[:, at], sems.at[len(copies)]))
        copies[-1].start()

    line = width // LANES * own
    small = (small_ref[...] + small2_ref[...]).astype(BF)
    out_ref[:, line:, :] = small.reshape(count, own // 2, LANES)
    send(line, line + own // 2)
    for n in range(width // part):
        at = slice(n * part, (n + 1) * part)
        total = jnp.dot(mine_ref[...], pack_ref[0:length, at], preferred_element_type=F32)
        total = total + jnp.dot(got, pack2_ref[0:length, at], preferred_element_type=F32)
        total = total.astype(BF).reshape(count, own, part)
        for b in range(part // LANES):
            line = (n * (part // LANES) + b) * own
            out_ref[:, line : line + own, :] = total[:, :, b * LANES : (b + 1) * LANES]
        send(n * (part // LANES) * own, (n + 1) * (part // LANES) * own)
    for copy in copies:
        copy.wait()


def taps_kernel(
    own, ga_ref, norm_ref, inv_ref, gain_ref, seg_ref, win,
    gm_hbm, mine_ref, other_ref, kacc, gg_ref, gm_ref, sems,
):
    length, width = norm_ref.shape
    taps = kacc.shape[0]
    blocks = width // LANES
    group = 4
    off = WIDE - taps // 2
    gg_ref[...] = jnp.zeros(gg_ref.shape, F32)
    kacc[...] = jnp.zeros(kacc.shape, F32)

    def rows_of(value):
        rows8 = value[0:8]
        for r in range(8, ROWS, 8):
            rows8 = rows8 + value[r : r + 8]
        return rows8

    def step(i, carry):
        r0 = pl.multiple_of(i * ROWS, ROWS)
        at = pl.ds(r0, ROWS)
        sum_a = jnp.zeros((ROWS, LANES), F32)
        sum_b = jnp.zeros((ROWS, LANES), F32)
        for b in range(blocks):
            lanes = slice(b * LANES, (b + 1) * LANES)
            gain = gain_ref[:, lanes]
            normed = norm_ref[at, lanes]
            gg = gate_back(ga_ref[at, lanes], normed, gain)
            gg_ref[:, lanes] = gg_ref[:, lanes] + rows_of(gg * normed)
            gn = gg * gain
            sum_a = sum_a + gn
            sum_b = sum_b + gn * normed
            gm_ref[at, lanes] = gn
        mean_a = jnp.sum(sum_a, axis=1, keepdims=True) * (1.0 / width)
        mean_b = jnp.sum(sum_b, axis=1, keepdims=True) * (1.0 / width)
        inv = inv_ref[at, :]
        centre = seg_ref[pl.ds(r0 + WIDE, ROWS), :]
        for g in range(blocks // group):
            grads = {}
            for b in range(g * group, (g + 1) * group):
                lanes = slice(b * LANES, (b + 1) * LANES)
                grads[b] = inv * (gm_ref[at, lanes] - mean_a - norm_ref[at, lanes] * mean_b)
                gm_ref[at, lanes] = grads[b]
            for shift in range(8):
                ks = range(shift, taps, 8)
                deep = ROWS + 8 * (len(ks) - 1)
                segs = seg_ref[pl.ds(r0 + off + shift, deep), :]
                wins = {b: win[b, pl.ds(r0 + off + shift, deep), :] for b in grads}
                for q, k in enumerate(ks):
                    same = segs[8 * q : 8 * q + ROWS] == centre
                    for b, grad in grads.items():
                        lanes = slice(b * LANES, (b + 1) * LANES)
                        prod = jnp.where(same, wins[b][8 * q : 8 * q + ROWS], 0.0) * grad
                        kacc[k, :, lanes] = kacc[k, :, lanes] + rows_of(prod)
        pltpu.make_async_copy(gm_ref.at[at], gm_hbm.at[at], sems.at[i]).start()
        return carry

    count = length // ROWS
    lax.fori_loop(0, count, step, 0)
    core = lax.axis_index("core")
    half = own // 2
    upper = (lax.broadcasted_iota(jnp.int32, (taps + 1, LANES), 1) // half) % 2 == 1
    for b in range(blocks):
        lanes = slice(b * LANES, (b + 1) * LANES)
        rows = [jnp.sum(kacc[k, :, lanes], axis=0, keepdims=True) for k in range(taps)]
        rows.append(jnp.sum(gg_ref[:, lanes], axis=0, keepdims=True))
        rows = jnp.concatenate(rows, axis=0)
        pad = jnp.zeros((LANES - 2 * (taps + 1), LANES), F32)
        turned = jnp.concatenate([jnp.where(upper, 0.0, rows), jnp.where(upper, rows, 0.0), pad], axis=0).T
        for j in range(LANES // (2 * own)):
            at = 2 * own * j
            even = turned[at : at + half] + turned[at + half : at + own]
            odd = turned[at + own : at + own + half] + turned[at + own + half : at + 2 * own]
            deal(core, (b * (LANES // (2 * own)) + j) * half, even, odd, mine_ref, other_ref)
    for i in range(count):
        at = pl.ds(i * ROWS, ROWS)
        pltpu.make_async_copy(gm_ref.at[at], gm_hbm.at[at], sems.at[i]).wait()


def back_kernel(
    pack_ref, proj_ref, gm_ref, mate_ref, outer_ref, seg_ref, kern_ref, gain_ref, hid_hbm,
    out_ref, gh_ref, gwin, hwin, hid_ref, ga_ref, sems,
):
    taps, width = kern_ref.shape
    length = gh_ref.shape[0]
    blocks = width // LANES
    copies = (
        pltpu.make_async_copy(hid_hbm.at[0:WIDE], hid_ref.at[0], sems.at[0]),
        pltpu.make_async_copy(hid_hbm.at[length - WIDE : length], hid_ref.at[1], sems.at[1]),
    )
    for copy in copies:
        copy.start()
    matmul_into(out_ref, ((pack_ref.at[0:length], proj_ref),), transposed=True)
    matmul_into(ga_ref.at[0:NEAR], ((mate_ref.at[WIDE:], proj_ref),))
    matmul_into(ga_ref.at[NEAR:], ((outer_ref.at[WIDE:], proj_ref),))
    for copy in copies:
        copy.wait()
    for b in range(blocks):
        lanes = slice(b * LANES, (b + 1) * LANES)
        gwin[b, NEAR : NEAR + length, :] = gm_ref[:, lanes]
        before, after = sorted_ends(mate_ref[0:WIDE, lanes].astype(F32), outer_ref[0:WIDE, lanes].astype(F32))
        hwin[b, 0:WIDE, :] = before
        hwin[b, WIDE : 2 * WIDE, :] = hid_ref[0, :, lanes].astype(F32)
        hwin[b, 2 * WIDE : 3 * WIDE, :] = hid_ref[1, :, lanes].astype(F32)
        hwin[b, 3 * WIDE :, :] = after
    reach = taps // 2
    sides = (
        (NEAR - reach, NEAR - reach, 0),
        (3 * WIDE - reach, WIDE + length - reach, NEAR + length),
    )
    for side, (wr, sr, to) in enumerate(sides):
        normed, inv = normalised(convolved(hwin, wr, seg_ref, sr, kern_ref, NEAR), width)
        grads = []
        for b in range(blocks):
            lanes = slice(b * LANES, (b + 1) * LANES)
            gain = gain_ref[:, lanes]
            grad = sorted_ends(ga_ref[0:NEAR, lanes], ga_ref[NEAR:, lanes])[side]
            grads.append(gate_back(grad, normed[b], gain) * gain)
        mean_a = mean_of(grads, width)
        mean_b = mean_of([g * n for g, n in zip(grads, normed)], width)
        for b in range(blocks):
            gwin[b, to : to + NEAR, :] = inv * (grads[b] - mean_a - normed[b] * mean_b)

    def step(i, carry):
        r0 = pl.multiple_of(i * ROWS, ROWS)
        acc = convolved(gwin, r0 + NEAR - reach, seg_ref, r0 + WIDE - reach, kern_ref, ROWS, True)
        for b in range(blocks):
            gh_ref[pl.ds(r0, ROWS), b * LANES : (b + 1) * LANES] = acc[b].astype(BF)
        return carry

    lax.fori_loop(0, length // ROWS, step, 0)


def add_kernel(landed_ref, out_ref):
    total = landed_ref[0].astype(F32)
    for j in range(1, landed_ref.shape[0]):
        total = total + landed_ref[j].astype(F32)
    out_ref[...] = total.astype(BF)


def final_kernel(factor, taps, all_ref, weight_ref, small_ref, gain_ref):
    total = all_ref[0].astype(F32)
    for j in range(1, all_ref.shape[0]):
        total = total + all_ref[j].astype(F32)
    total = total * factor
    own, width = weight_ref.shape
    for b in range(width // LANES):
        weight_ref[:, b * LANES : (b + 1) * LANES] = total[b * own : (b + 1) * own, :]
    tail = total[width // LANES * own :, :]
    tail = jnp.concatenate([tail[:, : taps + 1], tail[:, taps + 1 : 2 * (taps + 1)]], axis=0)
    small_ref[...] = tail[:, :taps]
    wide = jnp.concatenate([tail, jnp.zeros((own, LANES - taps - 1), F32)], axis=1)
    gain_ref[...] = wide.T[taps : taps + 1, :]


SEQ = ("y", "x", "core")


def inner(hidden, segment_ids, kernel, norm_gain, projection, cotangent):
    frames = hidden[0]
    length, width = frames.shape
    taps = kernel.shape[0]
    cot = cotangent[0]
    ny, nx = lax.axis_size("y"), lax.axis_size("x")
    seqs = ny * nx * 2
    own = width // seqs
    swap = [(0, 1), (1, 0)]
    big = 2 * length * width * width
    vec = length * width * taps
    shape = jax.ShapeDtypeStruct
    rows_win = length + 2 * WIDE
    blocks = width // LANES
    window = (blocks, rows_win, LANES)
    lines = (blocks * own) + own // 2

    message = shape((WIDE + NEAR, width), BF)
    to_mate, to_outer = call(
        ends_kernel, (message, message), [pltpu.SemaphoreType.DMA((4,))], moved=512 * width, hbm=(0, 1)
    )(frames, cot)
    mate = lax.ppermute(to_mate, "core", swap)
    outer = lax.ppermute(to_outer, SEQ, [(i, i + 1 if i % 2 else i - 1) for i in range(1, seqs - 1)])
    half = shape((width // 2, length), BF)
    ids = segment_ids.reshape(-1, LANES)
    mine, other, seg, mid, grad_act, kern, gain = call(
        partial(first_kernel, own),
        (
            half,
            half,
            shape((rows_win, LANES), F32),
            shape((blocks, length, LANES), F32),
            shape((length, width), F32),
            shape((taps, width), F32),
            shape((1, width), F32),
        ),
        [
            pltpu.VMEM(ids.shape, ids.dtype),
            pltpu.VMEM((length, width), BF),
            pltpu.VMEM((length, width), BF),
            pltpu.VMEM((width, width), BF),
            pltpu.SemaphoreType.DMA((6,)),
        ],
        flops=big,
        moved=12 * length * width,
        hbm=range(6),
    )(ids, cot, frames, projection, kernel, norm_gain[None, :])
    pack, normed, inv, win = call(
        forward_kernel,
        (
            shape((length + length // 2, width), BF),
            shape((length, width), F32),
            shape((length, LANES), F32),
            shape(window, F32),
        ),
        flops=3 * vec,
        moved=8 * length * width,
        trans=2 * length * width,
    )(mid, mate, outer, seg, kern, gain, other)
    pack2 = lax.ppermute(pack, "core", swap)
    dealt = shape((width // 4, LANES), F32)
    grad_mixed, small, small_other = call(
        partial(taps_kernel, own),
        (pltpu.HBM((length, width), F32), dealt, dealt),
        [
            pltpu.VMEM((taps, 8, width), F32),
            pltpu.VMEM((8, width), F32),
            pltpu.VMEM((length, width), F32),
            pltpu.SemaphoreType.DMA((length // ROWS,)),
        ],
        far=1,
        flops=3 * vec,
        moved=16 * length * width,
        trans=2 * length * width,
    )(grad_act, normed, inv, gain, seg, win)
    small2 = lax.ppermute(small_other, "core", swap)
    weight = call(
        partial(product_kernel, own),
        pltpu.HBM((ny * nx, lines, LANES), BF),
        [pltpu.VMEM((ny * nx, lines, LANES), BF), pltpu.SemaphoreType.DMA((width // 256 + 1,))],
        far=1,
        flops=big,
        moved=2 * (width * width + 3 * length * width),
    )(mine, pack, pack2, small, small2)
    landed = lax.all_to_all(weight, ("y", "x"), split_axis=0, concat_axis=0, tiled=True)
    conv_out, grad_hidden = call(
        back_kernel,
        (shape((length, width), BF), shape((length, width), BF)),
        [
            pltpu.VMEM((blocks, length + 2 * NEAR, LANES), F32),
            pltpu.VMEM((blocks, 4 * WIDE, LANES), F32),
            pltpu.VMEM((2, WIDE, width), BF),
            pltpu.VMEM((2 * NEAR, width), F32),
            pltpu.SemaphoreType.DMA((2,)),
        ],
        flops=3 * vec + big,
        moved=12 * length * width,
        hbm=(8,),
    )(pack, projection, grad_mixed, mate, outer, seg, kern, gain, frames)
    share = call(add_kernel, shape((lines, LANES), BF), moved=80 * own * width)(landed)
    everyone = lax.all_gather(share, "dp")
    factor = 1.0 / math.sqrt(length * ny * nx * 2 * lax.axis_size("dp"))
    grad_weight, grad_kernel, grad_gain = call(
        partial(final_kernel, factor, taps),
        (shape((own, width), F32), shape((own, taps), F32), shape((1, own), F32)),
        moved=64 * own * width,
    )(everyone)
    return conv_out[None], grad_hidden[None], grad_weight, grad_kernel, grad_gain[0]


def solution(mesh):
    dp, seq = mesh.devices.shape
    fine = Mesh(mesh.devices.reshape(dp, 8, seq // 16, 2), ("dp",) + SEQ)
    rows = P("dp", SEQ, None)
    in_specs = (rows, P("dp", None), P(), P(), P(), rows)
    out_specs = (rows, rows, P(SEQ, None), P(SEQ, None), P(SEQ))
    return jax.shard_map(inner, mesh=fine, in_specs=in_specs, out_specs=out_specs, check_vma=False)
```
